32 devices in a mesh: row: 4 (over y, x), col: 8 (over z, core).
Axes of the slice: x: 2, y: 2, z: 4, core: 2. Of those that a mesh axis runs over, the one named last changes fastest.
Arguments:
- rhs: bfloat16 [1024, 2, 4096], P('col', None, 'row'), may hold values from -6 to 6
- solved: bfloat16 [1024, 49152], P(None, 'col'), may hold values from -6 to 6
- panel: bfloat16 [2, 4096, 49152], P(None, 'row', 'col'), may hold values from -0.02734375 to 0.02734375
- inverse: bfloat16 [2, 4096, 4096], P(None, 'row'), as said below
- link: bfloat16 [4096, 4096], P('row'), may hold values from -0.09375 to 0.09375
Outputs:
- solution: bfloat16 [1024, 2, 4096], P('col', None, 'row')
The draws below stay inside these ranges and needn't reach their ends.
Inputs may be any that keep to these rules, and one draw needn't show every extreme that they name: Each inverse[b] is upper triangular with diagonal entries between 0.6 and 1.4.
All inputs are finite; a program needn't handle non-finite values.
Results may differ from the reference program's by a relative error of at most 0.0056.
Values may be sent and summed in bfloat16 or wider, within the bound.
No kernel may reach another device: no remote copies, remote signals or barrier semaphores. Data moves between devices by JAX's collectives and lax.ppermute only.
A program may use at most 128 MiB of HBM per device.

```python
import jax
import jax.numpy as jnp

BLOCK = 4096
SAMPLES = 1024
PRIOR = 49152


def draw_inverse(key, part):
    key_off = jax.random.fold_in(key, 11)
    key_diag = jax.random.fold_in(key, 12)
    values = jax.random.normal(key_off, (2, BLOCK, BLOCK), jnp.float32)
    rows_idx = jnp.arange(BLOCK)[:, None]
    cols_idx = jnp.arange(BLOCK)[None, :]
    upper = (rows_idx < cols_idx).astype(jnp.float32)
    same = (rows_idx == cols_idx).astype(jnp.float32)
    diag_vals = jax.random.uniform(key_diag, (2, 1, BLOCK), jnp.float32, 0.6, 1.4)
    scale = 0.8 / jnp.sqrt(jnp.float32(BLOCK))
    return (values * upper[None] * scale + same[None] * diag_vals).astype(jnp.bfloat16)


def strengthened(result, rng, source, target, blocks, factor):
    owner, partner = [(jnp.arange(result.shape[axis_at]) // (result.shape[axis_at] // blocks)).reshape([-1 if axis == axis_at else 1 for axis in range(result.ndim)]) for axis_at in (source, target)]
    chosen = jax.random.permutation(rng, blocks)[partner]
    strong = (owner == chosen) | (owner == (partner + blocks // 2) % blocks)
    return jnp.where(strong, factor * result, result)


def steps_of(rng, dims, shards, low, largest):
    gain = 1.0
    for axis_at, blocks in shards:
        heights = jax.random.uniform(jax.random.fold_in(jax.random.fold_in(rng, 6), axis_at), (blocks,), jnp.float32, low / len(shards), largest / len(shards))
        gain = gain * jnp.repeat(jnp.exp(heights), dims[axis_at] // blocks).reshape((-1,) + (1,) * (len(dims) - 1 - axis_at))
    return gain


def gaussian(stream_key, dims, scale, reach, pieces=(), kind=jnp.bfloat16):
    result = jax.random.normal(stream_key, dims, jnp.float32) * scale
    if len(pieces) > 0:
        result = steps_of(stream_key, dims, pieces, -0.22, 0.18) * result
    return jnp.clip(result, min=-reach, max=reach).astype(kind)


def gaussian_with(rng, shape, spread, most, split, heavy, dtype=jnp.bfloat16):
    values = spread * jax.random.normal(rng, shape, jnp.float32)
    if split:
        values = values * steps_of(rng, shape, split, -0.22, 0.18)
    return jnp.clip(strengthened(values, jax.random.fold_in(rng, 3), *heavy), -most, most).astype(dtype)


def setup_inputs(seed: int = 0) -> dict:
    key_list = jax.random.split(jax.random.key(seed), 6)
    rhs = gaussian(key_list[0], (SAMPLES, 2, BLOCK), 1.0, 6.0, ((0, 8), (2, 4)))
    solved = gaussian_with(key_list[1], (SAMPLES, PRIOR), 1.0, 6.0, ((1, 8),), (1, 0, 8, 2.0))
    panel = gaussian(key_list[2], (2, BLOCK, PRIOR), PRIOR ** -0.5, 0.02734375, ((1, 4), (2, 8)))
    inverse = draw_inverse(jax.random.fold_in(key_list[5], 71), 0)
    link = gaussian(key_list[4], (BLOCK, BLOCK), BLOCK ** -0.5, 0.09375, ((0, 4),))
    return dict(rhs=rhs, solved=solved, panel=panel, inverse=inverse, link=link)


def reference(rhs, solved, panel, inverse, link):
    flat_panel = panel.reshape(2 * BLOCK, PRIOR)
    sums = jnp.dot(solved, flat_panel.T, preferred_element_type=jnp.float32).reshape(SAMPLES, 2, BLOCK)
    first_res = (rhs[:, 0, :].astype(jnp.float32) - sums[:, 0, :]).astype(jnp.bfloat16)
    first = jnp.dot(first_res, inverse[0], preferred_element_type=jnp.float32).astype(jnp.bfloat16)
    carried = jnp.dot(first, link.T, preferred_element_type=jnp.float32)
    second_res = (rhs[:, 1, :].astype(jnp.float32) - sums[:, 1, :] - carried).astype(jnp.bfloat16)
    second = jnp.dot(second_res, inverse[1], preferred_element_type=jnp.float32).astype(jnp.bfloat16)
    return jnp.stack([first, second], axis=1)
```

```python
import functools

import jax
import jax.numpy as jnp
from jax import lax
from jax.experimental import pallas as pl
from jax.experimental.pallas import tpu as pltpu
from jax.sharding import PartitionSpec as P


F32, BF16 = jnp.float32, jnp.bfloat16
AHEAD = 3
PIECES = 4


def contract_last(a, b):
    return lax.dot_general(a, b, (((1,), (1,)), ((), ())), preferred_element_type=F32)


def tile_of(size, most):
    while size % most:
        most //= 2
    return most


def in_hbm(array):
    return pltpu.with_memory_space_constraint(array, pltpu.HBM)


def partial_kernel(block, half, tile, load_p, load_x, segments, fetched, *refs):
    refs = list(refs)
    starts, solved = refs.pop(0), refs.pop(0)
    x = None if load_x else refs.pop(0)
    panel = refs.pop(0)
    refs.pop(0)
    send, keep = refs.pop(0), refs.pop(0)
    held = refs.pop(0) if load_p else panel
    following = refs.pop(0) if fetched else None
    if load_x:
        x = refs.pop(0)
    acc, sems = refs
    depth = solved.shape[1]
    piece = depth // PIECES
    tiles = held.shape[0] // tile
    used = [0]

    def copy(source, target):
        used[0] += 1
        return pltpu.make_async_copy(source, target, sems.at[used[0] - 1])

    def rows_copy(slot, target, at, columns):
        start = pl.multiple_of(starts[slot], half)
        return copy(
            solved.at[pl.ds(start, half), columns], target.at[pl.ds(at * half, half), columns]
        )

    def panel_copy(n, columns):
        rows = pl.ds(n * tile, tile)
        return copy(panel.at[block, rows, columns], held.at[rows, columns])

    units = []
    if load_x or load_p:
        for j in range(PIECES):
            columns = pl.ds(j * piece, piece)
            unit = [rows_copy(s, x, s, columns) for s in range(segments)] if load_x else []
            units.append(unit + ([panel_copy(0, columns)] if load_p else []))
    if load_p:
        units += [[panel_copy(n, slice(None))] for n in range(1, tiles)]
    units += [[rows_copy(segments + s, following, s, slice(None))] for s in range(fetched)]
    begun, ended = [0], [0]

    def begin():
        while begun[0] < min(ended[0] + AHEAD, len(units)):
            for c in units[begun[0]]:
                c.start()
            begun[0] += 1

    def arrive():
        begin()
        for c in units[ended[0]]:
            c.wait()
        ended[0] += 1
        begin()

    begin()

    def put(d, n):
        at = pl.ds(pl.multiple_of(n * tile, tile), tile)
        count = segments // 2
        for c in range(count):
            send[c, :, at] = d[c * half : (c + 1) * half].astype(send.dtype)
            keep[c, :, at] = d[(count + c) * half : (count + c + 1) * half]

    def step(n, _):
        rows = pl.ds(pl.multiple_of(n * tile, tile), tile)
        put(contract_last(x[...], held[rows, :]), n)
        return 0

    first = 0
    if load_x or load_p:
        for j in range(PIECES):
            arrive()

            @pl.when(starts[0] >= 0)
            def _(j=j):
                columns = pl.ds(j * piece, piece)
                d = contract_last(x[:, columns], held[pl.ds(0, tile), columns])
                if j > 0:
                    d = acc[...] + d
                if j < PIECES - 1:
                    acc[...] = d
                else:
                    put(d, 0)

        first = 1
    if load_p:
        for n in range(first, tiles):
            arrive()

            @pl.when(starts[0] >= 0)
            def _(n=n):
                step(n, 0)

    else:
        lax.fori_loop(first, tiles, step, 0)
    while ended[0] < len(units):
        arrive()


def partial_sums(name, solved, x, panel, block, order, starts, following, half):
    load_x, load_p = x is None, panel.ndim == 3
    width, depth = panel.shape[-2:]
    segments, fetched = len(starts), len(following)
    rows, count = segments * half, segments // 2
    tile = tile_of(width, 256)
    hbm, vmem = pl.BlockSpec(memory_space=pltpu.HBM), pl.BlockSpec(memory_space=pltpu.VMEM)
    operands = [jnp.stack(starts + following).astype(jnp.int32), in_hbm(solved)]
    in_specs = [pl.BlockSpec(memory_space=pltpu.SMEM), hbm]
    if not load_x:
        operands.append(x)
        in_specs.append(vmem)
    operands += [in_hbm(panel) if load_p else panel, in_hbm(order)]
    in_specs += [hbm if load_p else vmem, hbm]
    shapes = [
        jax.ShapeDtypeStruct((count, half, width), BF16),
        jax.ShapeDtypeStruct((count, half, width), F32),
    ]
    if load_p:
        shapes.append(jax.ShapeDtypeStruct((width, depth), panel.dtype))
    if fetched:
        shapes.append(jax.ShapeDtypeStruct((fetched * half, depth), solved.dtype))
    scratch = [pltpu.VMEM((rows, depth), solved.dtype)] if load_x else []
    scratch.append(pltpu.VMEM((rows, tile), F32))
    copies = PIECES * (segments + 1) + width // tile + fetched
    scratch.append(pltpu.SemaphoreType.DMA((copies,)))
    out = pl.pallas_call(
        functools.partial(
            partial_kernel, block, half, tile, load_p, load_x, segments, fetched
        ),
        in_specs=in_specs,
        out_specs=[vmem] * len(shapes),
        out_shape=shapes,
        scratch_shapes=scratch,
        name=name,
        compiler_params=pltpu.CompilerParams(vmem_limit_bytes=12 << 20),
        cost_estimate=pl.CostEstimate(
            flops=2 * rows * width * depth,
            bytes_accessed=2 * depth * (rows + width),
            transcendentals=0,
        ),
    )(*operands)
    out = list(out)
    send, keep = out.pop(0), out.pop(0)
    held = out.pop(0) if load_p else panel
    return send, keep, held, out.pop(0) if fetched else None


def residual(b, rhs_ref, parts):
    total = parts[0][...].astype(F32)
    for part in parts[1:]:
        total += part[...].astype(F32)
    return rhs_ref[:, b, :].astype(F32) - total


def solve_first_kernel(count, mine, rhs, *refs):
    parts, inverse, outs, res = refs[:count], refs[count], refs[count + 1 : -1], refs[-1]
    k = pl.program_id(0)

    @pl.when(k == 0)
    def _():
        res[...] = residual(0, rhs, parts).astype(BF16)

    d = jnp.dot(res[...], inverse[0], preferred_element_type=F32)
    for at, out in enumerate(outs):

        @pl.when(k == at)
        def _(out=out):
            out[...] = d.astype(out.dtype)


def whole(shape):
    return pl.BlockSpec(shape, lambda k, mine: (0,) * len(shape))


def solve_first(rhs, parts, inverse, mine, members):
    half, _, width = rhs.shape
    block = whole((half, width))
    last = members - 1
    return pl.pallas_call(
        functools.partial(solve_first_kernel, len(parts)),
        grid_spec=pltpu.PrefetchScalarGridSpec(
            num_scalar_prefetch=1,
            grid=(members,),
            in_specs=[whole(rhs.shape)]
            + [block] * len(parts)
            + [pl.BlockSpec((1, width, width), lambda k, mine: (0, 0, mine[0] ^ (last - k)))],
            out_specs=[block] * members,
            scratch_shapes=[pltpu.VMEM((half, width), BF16)],
        ),
        out_shape=[jax.ShapeDtypeStruct((half, width), BF16)] * last
        + [jax.ShapeDtypeStruct((half, width), F32)],
        name="solve_first",
        compiler_params=pltpu.CompilerParams(vmem_limit_bytes=24 << 20),
        cost_estimate=pl.CostEstimate(
            flops=2 * half * width * width * members,
            bytes_accessed=2 * width * width * members,
            transcendentals=0,
        ),
    )(mine, rhs, *parts, in_hbm(inverse))


def solve_second_kernel(count, members, mine, rhs, *refs):
    parts, firsts = refs[:count], refs[count : count + members]
    link, inverse = refs[count + members : count + members + 2]
    outs, carried, res = refs[count + members + 2 : -2], refs[-2], refs[-1]
    k = pl.program_id(0)
    for at in range(members):

        @pl.when(k == at)
        def _(at=at):
            d = contract_last(firsts[at][...], link[...])
            if at > 0:
                d = carried[...] + d
            if at < members - 1:
                carried[...] = d
            else:
                res[...] = (residual(1, rhs, parts) - d).astype(BF16)

    for at, out in enumerate(outs):

        @pl.when(k == members + at)
        def _(out=out):
            d = jnp.dot(res[...], inverse[0], preferred_element_type=F32)
            out[...] = d.astype(out.dtype)


def solve_second(rhs, parts, firsts, link, inverse, mine, members):
    half, _, width = rhs.shape
    block = whole((half, width))
    last = members - 1
    return pl.pallas_call(
        functools.partial(solve_second_kernel, len(parts), members),
        grid_spec=pltpu.PrefetchScalarGridSpec(
            num_scalar_prefetch=1,
            grid=(2 * members,),
            in_specs=[whole(rhs.shape)]
            + [block] * (len(parts) + members)
            + [
                pl.BlockSpec(
                    (width, width), lambda k, mine: (0, mine[0] ^ jnp.minimum(k, last))
                ),
                pl.BlockSpec(
                    (1, width, width),
                    lambda k, mine: (1, 0, mine[0] ^ (last - jnp.maximum(k - members, 0))),
                ),
            ],
            out_specs=[block] * members,
            scratch_shapes=[pltpu.VMEM((half, width), F32), pltpu.VMEM((half, width), BF16)],
        ),
        out_shape=[jax.ShapeDtypeStruct((half, width), BF16)] * last
        + [jax.ShapeDtypeStruct((half, width), F32)],
        name="solve_second",
        compiler_params=pltpu.CompilerParams(vmem_limit_bytes=24 << 20),
        cost_estimate=pl.CostEstimate(
            flops=4 * half * width * width * members,
            bytes_accessed=4 * width * width * members,
            transcendentals=0,
        ),
    )(mine, rhs, *parts, *firsts, in_hbm(link), in_hbm(inverse))


def result_kernel(first, *refs):
    parts, out = refs[:-1], refs[-1]
    total = parts[0][...].astype(F32)
    for part in parts[1:]:
        total += part[...].astype(F32)
    out[:, 0, :] = first[...]
    out[:, 1, :] = total.astype(BF16)


def local(members, chips, rhs, solved, panel, inverse, link):
    half = rhs.shape[0]
    cols = 2 * chips
    mine = lax.axis_index("row")
    place = lax.axis_index("col")
    chip, core = place // 2, place % 2
    row_order = [mine.astype(jnp.int32)[None]]

    def across_row(value, offset):
        return lax.ppermute(value, "row", [(i, i ^ offset) for i in range(members)])

    def across_col(value, offset):
        return lax.ppermute(value, "col", [(i, i ^ offset) for i in range(cols)])

    def starts(group):
        def at(parity):
            return [((chip ^ o) * 2 + parity) * half for o in group]

        return at(1 - core) + at(core)

    pairs = [[o + 1, o] for o in range(chips - 2, -1, -2)]
    plan = [(0, g) for g in [[o] for o in pairs[0]] + pairs[1:]] + [(1, g) for g in pairs]
    if chips == 1:
        plan = [(0, [0]), (1, [0])]

    sums = [[], []]
    x, held = None, None
    orders = [solved]
    for n, (b, group) in enumerate(plan):
        fresh = n == 0 or plan[n - 1][0] != b
        following = starts(plan[n + 1][1]) if n + 1 < len(plan) else []
        source = panel if fresh else held
        send, keep, held, x = partial_sums(
            f"sums_{b}_{n}", solved, x, source, b, orders[max(0, n - 1)], starts(group), following, half
        )
        other = across_col(send, 1)
        outgoing = None
        for at, offset in enumerate(group):
            if offset == 0:
                sums[b] += [keep[at], other[at]]
            else:
                outgoing = (keep[at] + other[at].astype(F32)).astype(BF16)
                sums[b].append(across_col(outgoing, 2 * offset))
        orders.append(outgoing if outgoing is not None else keep)

    parts = solve_first(rhs, sums[0], inverse, row_order[0], members)
    total = parts[-1]
    for at in range(members - 1):
        total += across_row(parts[at], members - 1 - at).astype(F32)
    first = total.astype(BF16)
    firsts = [first] + [across_row(first, o) for o in range(1, members)]
    parts = solve_second(rhs, sums[1], firsts, link, inverse, row_order[0], members)
    arrived = [across_row(parts[at], members - 1 - at) for at in range(members - 1)]
    return pl.pallas_call(
        result_kernel,
        out_shape=jax.ShapeDtypeStruct(rhs.shape, rhs.dtype),
        name="result",
    )(first, parts[-1], *arrived)


def solution(mesh):
    members, cols = mesh.shape["row"], mesh.shape["col"]
    return jax.shard_map(
        functools.partial(local, members, cols // 2),
        mesh=mesh,
        in_specs=(
            P("col", None, "row"),
            P(None, "col"),
            P(None, "row", "col"),
            P(None, "row", None),
            P("row", None),
        ),
        out_specs=P("col", None, "row"),
        check_vma=False,
    )
```

```python
import functools

import jax
import jax.numpy as jnp
from jax import lax
from jax.experimental import pallas as pl
from jax.experimental.pallas import tpu as pltpu
from jax.sharding import PartitionSpec as P


F32, BF16 = jnp.float32, jnp.bfloat16
AHEAD = 3
PIECES = 4
LIMIT = 8 << 20


def contract_last(a, b):
    return lax.dot_general(a, b, (((1,), (1,)), ((), ())), preferred_element_type=F32)


def tile_of(size, most):
    while size % most:
        most //= 2
    return most


def in_hbm(array):
    return pltpu.with_memory_space_constraint(array, pltpu.HBM)


def partial_kernel(cfg, *refs):
    block, half, tile, load_p, load_x, group, following, ordered, extras, chips = cfg
    refs = list(refs)
    place, solved = refs.pop(0)[0], refs.pop(0)
    x = None if load_x else refs.pop(0)
    panel = refs.pop(0)
    if ordered:
        refs.pop(0)
    wanted = [refs.pop(0) for _ in extras]
    send, keep = refs.pop(0), refs.pop(0)
    held = refs.pop(0) if load_p else panel
    upcoming = refs.pop(0) if following else None
    fetched = [refs.pop(0) for _ in extras]
    if load_x:
        x = refs.pop(0)
    acc, sems = refs
    depth = solved.shape[1]
    piece = depth // PIECES
    tiles = held.shape[0] // tile
    count = len(group)
    chip, core = lax.rem(place, 2 * chips) // 2, lax.rem(place, 2)
    used = [0]

    def copy(source, target):
        used[0] += 1
        return pltpu.make_async_copy(source, target, sems.at[used[0] - 1])

    def rows_copy(offsets, target, at, columns):
        parity = 1 - core if at < len(offsets) else core
        start = ((chip ^ offsets[at % len(offsets)]) * 2 + parity) * half
        return copy(
            solved.at[pl.ds(pl.multiple_of(start, half), half), columns],
            target.at[pl.ds(at * half, half), columns],
        )

    def panel_copy(n, columns):
        rows = pl.ds(n * tile, tile)
        return copy(panel.at[block, rows, columns], held.at[rows, columns])

    units = []
    if load_x or load_p:
        for j in range(PIECES):
            columns = pl.ds(j * piece, piece)
            unit = [rows_copy(group, x, s, columns) for s in range(2 * count)] if load_x else []
            units.append(unit + ([panel_copy(0, columns)] if load_p else []))
    if load_p:
        units += [[panel_copy(n, slice(None))] for n in range(1, tiles)]
    units += [[rows_copy(following, upcoming, s, slice(None))] for s in range(2 * len(following))]
    for (_, layer), source, target in zip(extras, wanted, fetched):
        step = target.shape[0] // PIECES
        for j in range(PIECES):
            rows = pl.ds(j * step, step)
            units.append([copy(source.at[rows] if layer is None else source.at[layer, rows], target.at[rows])])
    begun, ended = [0], [0]

    def begin():
        while begun[0] < min(ended[0] + AHEAD, len(units)):
            for c in units[begun[0]]:
                c.start()
            begun[0] += 1

    def arrive():
        begin()
        for c in units[ended[0]]:
            c.wait()
        ended[0] += 1
        begin()

    begin()

    def put(d, n):
        at = pl.ds(pl.multiple_of(n * tile, tile), tile)
        for c in range(count):
            send[c, :, at] = d[c * half : (c + 1) * half].astype(send.dtype)
            keep[c, :, at] = d[(count + c) * half : (count + c + 1) * half]

    def step(n):
        rows = pl.ds(pl.multiple_of(n * tile, tile), tile)
        put(contract_last(x[...], held[rows, :]), n)

    first = 0
    if load_x or load_p:
        for j in range(PIECES):
            arrive()

            @pl.when(place >= 0)
            def _(j=j):
                columns = pl.ds(j * piece, piece)
                d = contract_last(x[:, columns], held[pl.ds(0, tile), columns])
                if j > 0:
                    d = acc[...] + d
                if j < PIECES - 1:
                    acc[...] = d
                else:
                    put(d, 0)

        first = 1
    for n in range(first, tiles):
        if load_p or (ended[0] < len(units) and n > first):
            arrive()

        @pl.when(place >= 0)
        def _(n=n):
            step(n)

    while ended[0] < len(units):
        arrive()


def partial_sums(name, solved, x, panel, block, order, place, group, following, half, chips, extras):
    load_x, load_p = x is None, panel.ndim == 3
    width, depth = panel.shape[-2:]
    count = len(group)
    rows = 2 * count * half
    tile = tile_of(width, 256)
    hbm, vmem = pl.BlockSpec(memory_space=pltpu.HBM), pl.BlockSpec(memory_space=pltpu.VMEM)
    operands = [place, in_hbm(solved)]
    in_specs = [pl.BlockSpec(memory_space=pltpu.SMEM), hbm]
    if not load_x:
        operands.append(x)
        in_specs.append(vmem)
    operands.append(in_hbm(panel) if load_p else panel)
    in_specs.append(hbm if load_p else vmem)
    if order is not None:
        operands.append(order)
        in_specs.append(pl.BlockSpec(memory_space=pl.ANY))
    operands += [in_hbm(array) for array, _ in extras]
    in_specs += [hbm] * len(extras)
    shapes = [
        jax.ShapeDtypeStruct((count, half, width), BF16),
        jax.ShapeDtypeStruct((count, half, width), F32),
    ]
    if load_p:
        shapes.append(jax.ShapeDtypeStruct((width, depth), panel.dtype))
    if following:
        shapes.append(jax.ShapeDtypeStruct((2 * len(following) * half, depth), solved.dtype))
    shapes += [jax.ShapeDtypeStruct(array.shape[-2:], array.dtype) for array, _ in extras]
    scratch = [pltpu.VMEM((rows, depth), solved.dtype)] if load_x else []
    scratch.append(pltpu.VMEM((rows, tile), F32))
    copies = PIECES * (2 * count + 1) + width // tile + 2 * len(following) + PIECES * len(extras)
    scratch.append(pltpu.SemaphoreType.DMA((copies,)))
    cfg = (
        block, half, tile, load_p, load_x, tuple(group), tuple(following), order is not None,
        tuple((None, layer) for _, layer in extras), chips,
    )
    out = pl.pallas_call(
        functools.partial(partial_kernel, cfg),
        in_specs=in_specs,
        out_specs=[vmem] * len(shapes),
        out_shape=shapes,
        scratch_shapes=scratch,
        name=name,
        compiler_params=pltpu.CompilerParams(vmem_limit_bytes=LIMIT),
        cost_estimate=pl.CostEstimate(
            flops=2 * rows * width * depth,
            bytes_accessed=2 * depth * (rows + width),
            transcendentals=0,
        ),
    )(*operands)
    out = list(out)
    send, keep = out.pop(0), out.pop(0)
    held = out.pop(0) if load_p else panel
    return send, keep, held, out.pop(0) if following else None, out


def residual(b, rhs_ref, parts):
    total = parts[0][...].astype(F32)
    for part in parts[1:]:
        total += part[...].astype(F32)
    return rhs_ref[:, b, :].astype(F32) - total


def blocks_of(mine, members, width):
    return [
        pl.ds(pl.multiple_of((mine ^ offset) * width, width), width)
        for offset in range(members)
    ]


def solve_first_kernel(count, cols, place, rhs, *refs):
    parts, inverse, outs = refs[:count], refs[count], refs[count + 1 :]
    members, width = len(outs), rhs.shape[2]
    at = blocks_of(place[0] // cols, members, width)
    res = residual(0, rhs, parts).astype(BF16)
    for offset in range(members - 1, -1, -1):
        d = jnp.dot(res, inverse[:, at[offset]], preferred_element_type=F32)
        outs[offset][...] = d.astype(outs[offset].dtype)


def solve_second_kernel(count, members, cols, place, rhs, *refs):
    parts, firsts = refs[:count], refs[count : count + members]
    link, inverse = refs[count + members : count + members + 2]
    outs = refs[count + members + 2 :]
    at = blocks_of(place[0] // cols, members, rhs.shape[2])
    carried = contract_last(firsts[0][...], link[:, at[0]])
    for offset in range(1, members):
        carried += contract_last(firsts[offset][...], link[:, at[offset]])
    res = (residual(1, rhs, parts) - carried).astype(BF16)
    for offset in range(members - 1, -1, -1):
        d = jnp.dot(res, inverse[:, at[offset]], preferred_element_type=F32)
        outs[offset][...] = d.astype(outs[offset].dtype)


def solve(name, kernel, flops, place, rhs, parts, rest, members):
    half, _, width = rhs.shape
    vmem = pl.BlockSpec(memory_space=pltpu.VMEM)
    shapes = [
        jax.ShapeDtypeStruct((half, width), BF16 if offset else F32) for offset in range(members)
    ]
    return pl.pallas_call(
        kernel,
        in_specs=[pl.BlockSpec(memory_space=pltpu.SMEM)] + [vmem] * (1 + len(parts) + len(rest)),
        out_specs=[vmem] * members,
        out_shape=shapes,
        name=name,
        compiler_params=pltpu.CompilerParams(vmem_limit_bytes=LIMIT),
        cost_estimate=pl.CostEstimate(flops=flops, bytes_accessed=flops // half, transcendentals=0),
    )(place, rhs, *parts, *rest)


def result_kernel(first, *refs):
    parts, out = refs[:-1], refs[-1]
    total = parts[0][...].astype(F32)
    for part in parts[1:]:
        total += part[...].astype(F32)
    out[:, 0, :] = first[...]
    out[:, 1, :] = total.astype(BF16)


def local(members, chips, rhs, solved, panel, inverse, link):
    half, _, width = rhs.shape
    cols = 2 * chips
    place = lax.axis_index(("row", "col")).astype(jnp.int32)[None]

    def across_row(value, offset):
        return lax.ppermute(value, "row", [(i, i ^ offset) for i in range(members)])

    def across_col(value, offset):
        return lax.ppermute(value, "col", [(i, i ^ offset) for i in range(cols)])

    plan = [(0, [o]) for o in range(chips - 1, -1, -1)]
    plan += [(1, [o + 1, o] if chips > 1 else [o]) for o in range(max(chips - 2, 0), -1, -2)]
    last = len(plan) - 1

    sums, orders, extra = [[], []], [None], []
    x, held = None, None
    for n, (b, group) in enumerate(plan):
        fresh = n == 0 or plan[n - 1][0] != b
        following = plan[n + 1][1] if n < last else []
        order = orders[max(0, n - 1)]
        extras = []
        if n == chips - 1:
            extras = [(inverse, 0)]
        if n == last:
            flops = 2 * half * width * width * members
            parts = solve(
                "solve_first",
                functools.partial(solve_first_kernel, len(sums[0]), cols),
                flops, place, rhs, sums[0], extra, members,
            )
            order = parts[1] if members > 1 else parts[0]
            extras = [(link, None), (inverse, 1)]
        send, keep, held, x, got = partial_sums(
            f"sums_{b}_{n}", solved, x, panel if fresh else held, b, order, place,
            group, following, half, chips, extras,
        )
        extra = got if got else extra
        other = across_col(send, 1)
        outgoing = None
        for at, offset in enumerate(group):
            if offset == 0:
                sums[b] += [keep[at], other[at]]
            else:
                outgoing = (keep[at] + other[at].astype(F32)).astype(BF16)
                sums[b].append(across_col(outgoing, 2 * offset))
        orders.append(outgoing if outgoing is not None else keep)

    total = parts[0]
    for offset in range(1, members):
        total += across_row(parts[offset], offset).astype(F32)
    first = total.astype(BF16)
    firsts = [first] + [across_row(first, o) for o in range(1, members)]
    parts = solve(
        "solve_second",
        functools.partial(solve_second_kernel, len(sums[1]), members, cols),
        2 * flops, place, rhs, sums[1], firsts + extra, members,
    )
    arrived = [across_row(parts[offset], offset) for offset in range(1, members)]
    return pl.pallas_call(
        result_kernel,
        out_shape=jax.ShapeDtypeStruct(rhs.shape, rhs.dtype),
        name="result",
        compiler_params=pltpu.CompilerParams(vmem_limit_bytes=LIMIT),
    )(first, parts[0], *arrived)


def solution(mesh):
    members, cols = mesh.shape["row"], mesh.shape["col"]
    return jax.shard_map(
        functools.partial(local, members, cols // 2),
        mesh=mesh,
        in_specs=(
            P("col", None, "row"),
            P(None, "col"),
            P(None, "row", "col"),
            P(None, "row", None),
            P("row", None),
        ),
        out_specs=P("col", None, "row"),
        check_vma=False,
    )
```

```python
import functools

import jax
import jax.numpy as jnp
from jax import lax
from jax.experimental import pallas as pl
from jax.experimental.pallas import tpu as pltpu
from jax.sharding import PartitionSpec as P


F32, BF16 = jnp.float32, jnp.bfloat16
AHEAD = 3
PIECES = 4
LIMIT = 8 << 20


def contract_last(a, b):
    return lax.dot_general(a, b, (((1,), (1,)), ((), ())), preferred_element_type=F32)


def tile_of(size, most):
    while size % most:
        most //= 2
    return most


def in_hbm(array):
    return pltpu.with_memory_space_constraint(array, pltpu.HBM)


def partial_kernel(cfg, *refs):
    block, half, tile, load_p, load_x, group, following, ordered, blocks, extras, chips = cfg
    refs = list(refs)
    place, solved = refs.pop(0)[0], refs.pop(0)
    x = None if load_x else refs.pop(0)
    held = [refs.pop(0) for _ in range(blocks)]
    panel = held[0]
    for _ in range(ordered):
        refs.pop(0)
    wanted = [refs.pop(0) for _ in extras]
    send, keep = refs.pop(0), refs.pop(0)
    if load_p:
        held = [refs.pop(0)]
    upcoming = refs.pop(0) if following else None
    fetched = [refs.pop(0) for _ in extras]
    if load_x:
        x = refs.pop(0)
    acc, sems = refs
    depth = solved.shape[1]
    piece = depth // PIECES
    per = held[0].shape[0] // tile
    tiles = per * len(held)
    count = len(group)
    chip, core = lax.rem(place, 2 * chips) // 2, lax.rem(place, 2)
    used = [0]

    def copy(source, target):
        used[0] += 1
        return pltpu.make_async_copy(source, target, sems.at[used[0] - 1])

    def rows_copy(offsets, target, at, columns):
        parity = 1 - core if at < len(offsets) else core
        start = ((chip ^ offsets[at % len(offsets)]) * 2 + parity) * half
        return copy(
            solved.at[pl.ds(pl.multiple_of(start, half), half), columns],
            target.at[pl.ds(at * half, half), columns],
        )

    def panel_copy(n, columns):
        rows = pl.ds(n * tile, tile)
        return copy(panel.at[block, rows, columns], held[0].at[rows, columns])

    units = []
    if load_x or load_p:
        for j in range(PIECES):
            columns = pl.ds(j * piece, piece)
            unit = [rows_copy(group, x, s, columns) for s in range(2 * count)] if load_x else []
            units.append(unit + ([panel_copy(0, columns)] if load_p else []))
    if load_p:
        units += [[panel_copy(n, slice(None))] for n in range(1, tiles)]
    units += [[rows_copy(following, upcoming, s, slice(None))] for s in range(2 * len(following))]
    for (layer, low), source, target in zip(extras, wanted, fetched):
        step = target.shape[0] // PIECES
        for j in range(PIECES):
            rows = pl.ds(low + j * step, step)
            part = source.at[rows] if layer is None else source.at[layer, rows]
            units.append([copy(part, target.at[pl.ds(j * step, step)])])
    ahead = AHEAD if load_p else len(units)
    begun, ended = [0], [0]

    def begin():
        while begun[0] < min(ended[0] + ahead, len(units)):
            for c in units[begun[0]]:
                c.start()
            begun[0] += 1

    def arrive():
        begin()
        for c in units[ended[0]]:
            c.wait()
        ended[0] += 1
        begin()

    begin()

    def put(d, n):
        at = pl.ds(n * tile, tile)
        for c in range(count):
            send[c, :, at] = d[c * half : (c + 1) * half].astype(send.dtype)
            keep[c, :, at] = d[(count + c) * half : (count + c + 1) * half]

    def step(n):
        put(contract_last(x[...], held[n // per][pl.ds(n % per * tile, tile), :]), n)

    first = 0
    if load_x or load_p:
        for j in range(PIECES):
            arrive()

            @pl.when(place >= 0)
            def _(j=j):
                columns = pl.ds(j * piece, piece)
                d = contract_last(x[:, columns], held[0][pl.ds(0, tile), columns])
                if j > 0:
                    d = acc[...] + d
                if j < PIECES - 1:
                    acc[...] = d
                else:
                    put(d, 0)

        first = 1
    for n in range(first, tiles):
        if load_p:
            arrive()

        @pl.when(place >= 0)
        def _(n=n):
            step(n)

    while ended[0] < len(units):
        arrive()


def partial_sums(solved, x, panel, block, orders, place, group, following, half, chips, extras):
    load_x, load_p = x is None, not isinstance(panel, list)
    panels = [in_hbm(panel)] if load_p else panel
    depth = solved.shape[1]
    width = panel.shape[1] if load_p else sum(part.shape[0] for part in panel)
    count = len(group)
    rows = 2 * count * half
    tile = tile_of(width // 2, 256)
    hbm, vmem = pl.BlockSpec(memory_space=pltpu.HBM), pl.BlockSpec(memory_space=pltpu.VMEM)
    operands = [place, in_hbm(solved)]
    in_specs = [pl.BlockSpec(memory_space=pltpu.SMEM), hbm]
    if not load_x:
        operands.append(x)
        in_specs.append(vmem)
    operands += panels
    in_specs += [hbm if load_p else vmem] * len(panels)
    operands += orders
    in_specs += [pl.BlockSpec(memory_space=pl.ANY)] * len(orders)
    operands += [in_hbm(array) for array, *_ in extras]
    in_specs += [hbm] * len(extras)
    shapes = [
        jax.ShapeDtypeStruct((count, half, width), BF16),
        jax.ShapeDtypeStruct((count, half, width), F32),
    ]
    if load_p:
        shapes.append(jax.ShapeDtypeStruct((width, depth), panel.dtype))
    if following:
        shapes.append(jax.ShapeDtypeStruct((2 * len(following) * half, depth), solved.dtype))
    shapes += [
        jax.ShapeDtypeStruct((size, array.shape[-1]), array.dtype) for array, _, _, size in extras
    ]
    scratch = [pltpu.VMEM((rows, depth), solved.dtype)] if load_x else []
    scratch.append(pltpu.VMEM((rows, tile), F32))
    copies = PIECES * (2 * count + 1) + width // tile + 2 * len(following) + PIECES * len(extras)
    scratch.append(pltpu.SemaphoreType.DMA((copies,)))
    cfg = (
        block, half, tile, load_p, load_x, tuple(group), tuple(following), len(orders),
        len(panels), tuple((layer, low) for _, layer, low, _ in extras), chips,
    )
    out = pl.pallas_call(
        functools.partial(partial_kernel, cfg),
        in_specs=in_specs,
        out_specs=[vmem] * len(shapes),
        out_shape=shapes,
        scratch_shapes=scratch,
        compiler_params=pltpu.CompilerParams(vmem_limit_bytes=LIMIT),
        cost_estimate=pl.CostEstimate(
            flops=2 * rows * width * depth,
            bytes_accessed=2 * depth * (rows + width),
            transcendentals=0,
        ),
    )(*operands)
    out = list(out)
    send, keep = out.pop(0), out.pop(0)
    held = [out.pop(0)] if load_p else panel
    return send, keep, held, out.pop(0) if following else None, out


def residual(b, rhs_ref, parts):
    total = parts[0][...].astype(F32)
    for part in parts[1:]:
        total += part[...].astype(F32)
    return rhs_ref[:, b, :].astype(F32) - total


def blocks_of(mine, members, width):
    return [
        pl.ds(pl.multiple_of((mine ^ offset) * width, width), width)
        for offset in range(members)
    ]


def solve_first_kernel(count, cols, place, rhs, *refs):
    parts, inverse, outs = refs[:count], refs[count], refs[count + 1 :]
    members, width = len(outs), rhs.shape[2]
    at = blocks_of(place[0] // cols, members, width)
    res = residual(0, rhs, parts).astype(BF16)
    for offset in range(members - 1, -1, -1):
        d = jnp.dot(res, inverse[:, at[offset]], preferred_element_type=F32)
        outs[offset][...] = d.astype(outs[offset].dtype)


def carry(firsts, link, at, offsets):
    total = None
    for first, offset in zip(firsts, offsets):
        d = contract_last(first[...], link[:, at[offset]])
        total = d if total is None else total + d
    return total


def carry_kernel(members, offsets, cols, place, *refs):
    firsts, link, out = refs[:-2], refs[-2], refs[-1]
    at = blocks_of(place[0] // cols, members, out.shape[1])
    out[...] = carry(firsts, link, at, offsets)


def solve_second_kernel(count, members, offsets, cols, place, rhs, *refs):
    parts, refs = refs[:count], refs[count:]
    early, refs = refs[0], refs[1:]
    firsts, refs = refs[: len(offsets)], refs[len(offsets) :]
    link, inverse, outs = refs[0], refs[1], refs[2:]
    at = blocks_of(place[0] // cols, members, rhs.shape[2])
    carried = early[...]
    if offsets:
        carried += carry(firsts, link, at, offsets)
    res = (residual(1, rhs, parts) - carried).astype(BF16)
    for offset in range(members - 1, -1, -1):
        d = jnp.dot(res, inverse[:, at[offset]], preferred_element_type=F32)
        outs[offset][...] = d.astype(outs[offset].dtype)


def solve(kernel, flops, place, rhs, parts, rest, members):
    half, _, width = rhs.shape
    vmem = pl.BlockSpec(memory_space=pltpu.VMEM)
    shapes = [
        jax.ShapeDtypeStruct((half, width), BF16 if offset else F32) for offset in range(members)
    ]
    return pl.pallas_call(
        kernel,
        in_specs=[pl.BlockSpec(memory_space=pltpu.SMEM)] + [vmem] * (1 + len(parts) + len(rest)),
        out_specs=[vmem] * members,
        out_shape=shapes,
        compiler_params=pltpu.CompilerParams(vmem_limit_bytes=LIMIT),
        cost_estimate=pl.CostEstimate(flops=flops, bytes_accessed=flops // half, transcendentals=0),
    )(place, rhs, *parts, *rest)


def result_kernel(first, *refs):
    parts, out = refs[:-1], refs[-1]
    total = parts[0][...].astype(F32)
    for part in parts[1:]:
        total += part[...].astype(F32)
    out[:, 0, :] = first[...]
    out[:, 1, :] = total.astype(BF16)


def plan_of(chips):
    plan = [(0, [o]) for o in range(chips - 1, -1, -1)]
    return plan + [(1, [o + 1, o] if chips > 1 else [o]) for o in range(max(chips - 2, 0), -1, -2)]


def local(members, chips, rhs, solved, panel, inverse, link):
    half, _, width = rhs.shape
    cols = 2 * chips
    place = lax.axis_index(("row", "col")).astype(jnp.int32)[None]

    def across_row(value, offset):
        return lax.ppermute(value, "row", [(i, i ^ offset) for i in range(members)])

    def across_col(value, offset):
        return lax.ppermute(value, "col", [(i, i ^ offset) for i in range(cols)])

    plan = plan_of(chips)
    last = len(plan) - 1

    extras = [[] for _ in plan]
    extras[chips].append(("inverse", inverse, 0, 0, width))
    piece = width // 2
    extras[max(0, chips - 2)].append(("low", panel, 1, 0, piece))
    extras[chips - 1].append(("high", panel, 1, piece, piece))
    extras[last].append(("link", link, None, 0, width))
    extras[last].append(("second", inverse, 1, 0, width))

    flops = 2 * half * width * width * members
    sums, sent, kept = [[], []], [], {}
    x, held = None, panel
    for n, (b, group) in enumerate(plan):
        if b == 1 and plan[n - 1][0] == 0:
            held = [kept["low"], kept["high"]]
        following = plan[n + 1][1] if n < last else []
        orders = sent[n - 2] if n >= 2 else []
        if n == last:
            parts = solve(
                functools.partial(solve_first_kernel, len(sums[0]), cols),
                flops, place, rhs, sums[0], [kept["inverse"]], members,
            )
            orders = sent[n - 1] + [parts[members > 1]]
        send, keep, held, x, got = partial_sums(
            solved, x, held, b, orders, place,
            group, following, half, chips, [e[1:] for e in extras[n]],
        )
        kept.update(zip([e[0] for e in extras[n]], got))
        other = across_col(send, 1)
        outgoing = []
        for at, offset in enumerate(group):
            if offset == 0:
                sums[b] += [keep[at], other[at]]
            else:
                outgoing.append((keep[at] + other[at].astype(F32)).astype(BF16))
                sums[b].append(across_col(outgoing[-1], 2 * offset))
        sent.append(outgoing)

    total = parts[0]
    for offset in range(1, members):
        total += across_row(parts[offset], offset).astype(F32)
    first = total.astype(BF16)
    firsts = [first] + [across_row(first, o) for o in range(1, members)]
    early = sorted({0, members // 2 if members > 2 else 0})
    late = [o for o in range(members) if o not in early]
    vmem = pl.BlockSpec(memory_space=pltpu.VMEM)
    carried = pl.pallas_call(
        functools.partial(carry_kernel, members, early, cols),
        in_specs=[pl.BlockSpec(memory_space=pltpu.SMEM)] + [vmem] * (1 + len(early)),
        out_specs=vmem,
        out_shape=jax.ShapeDtypeStruct((half, width), F32),
        name="carry",
        compiler_params=pltpu.CompilerParams(vmem_limit_bytes=LIMIT),
        cost_estimate=pl.CostEstimate(
            flops=2 * half * width * width, bytes_accessed=width * width, transcendentals=0
        ),
    )(place, *[firsts[o] for o in early], kept["link"])
    parts = solve(
        functools.partial(solve_second_kernel, len(sums[1]), members, late, cols),
        2 * flops, place, rhs, sums[1],
        [carried] + [firsts[o] for o in late] + [kept["link"], kept["second"]], members,
    )
    arrived = [across_row(parts[offset], offset) for offset in range(1, members)]
    return pl.pallas_call(
        result_kernel,
        out_shape=jax.ShapeDtypeStruct(rhs.shape, rhs.dtype),
        name="result",
        compiler_params=pltpu.CompilerParams(vmem_limit_bytes=LIMIT),
    )(first, parts[0], *arrived)


def solution(mesh):
    members, chips = mesh.shape["row"], mesh.shape["col"] // 2

    def body(*arrays):
        return local(members, chips, *arrays)

    return jax.shard_map(
        body,
        mesh=mesh,
        in_specs=(
            P("col", None, "row"),
            P(None, "col"),
            P(None, "row", "col"),
            P(None, "row", None),
            P("row", None),
        ),
        out_specs=P("col", None, "row"),
        check_vma=False,
    )
```

```python
import functools

import jax
import jax.numpy as jnp
from jax import lax
from jax.experimental import pallas as pl
from jax.experimental.pallas import tpu as pltpu
from jax.sharding import PartitionSpec as P


F32, BF16 = jnp.float32, jnp.bfloat16
AHEAD = 3
PIECES = 4
LIMIT = 8 << 20


def contract_last(a, b):
    return lax.dot_general(a, b, (((1,), (1,)), ((), ())), preferred_element_type=F32)


def tile_of(size, most):
    while size % most:
        most //= 2
    return most


def in_hbm(array):
    return pltpu.with_memory_space_constraint(array, pltpu.HBM)


def partial_kernel(cfg, *refs):
    block, half, tile, load_p, load_x, group, following, ordered, blocks, extras, chips = cfg
    refs = list(refs)
    place, solved = refs.pop(0)[0], refs.pop(0)
    x = None if load_x else refs.pop(0)
    held = [refs.pop(0) for _ in range(blocks)]
    panel = held[0]
    for _ in range(ordered):
        refs.pop(0)
    wanted = [refs.pop(0) for _ in extras]
    send, keep = refs.pop(0), refs.pop(0)
    if load_p:
        held = [refs.pop(0)]
    upcoming = refs.pop(0) if following else None
    fetched = [refs.pop(0) for _ in extras]
    if load_x:
        x = refs.pop(0)
    acc, sems = refs
    depth = solved.shape[1]
    piece = depth // PIECES
    per = held[0].shape[0] // tile
    tiles = per * len(held)
    count = len(group)
    chip, core = lax.rem(place, 2 * chips) // 2, lax.rem(place, 2)
    used = [0]

    def copy(source, target):
        used[0] += 1
        return pltpu.make_async_copy(source, target, sems.at[used[0] - 1])

    def rows_copy(offsets, target, at, columns):
        parity = 1 - core if at < len(offsets) else core
        start = ((chip ^ offsets[at % len(offsets)]) * 2 + parity) * half
        return copy(
            solved.at[pl.ds(pl.multiple_of(start, half), half), columns],
            target.at[pl.ds(at * half, half), columns],
        )

    def panel_copy(n, columns):
        rows = pl.ds(n * tile, tile)
        return copy(panel.at[block, rows, columns], held[0].at[rows, columns])

    units = []
    if load_x or load_p:
        for j in range(PIECES):
            columns = pl.ds(j * piece, piece)
            unit = [rows_copy(group, x, s, columns) for s in range(2 * count)] if load_x else []
            units.append(unit + ([panel_copy(0, columns)] if load_p else []))
    if load_p:
        units += [[panel_copy(n, slice(None))] for n in range(1, tiles)]
    units += [[rows_copy(following, upcoming, s, slice(None))] for s in range(2 * len(following))]
    for (layer, low), source, target in zip(extras, wanted, fetched):
        step = target.shape[0] // PIECES
        for j in range(PIECES):
            rows = pl.ds(low + j * step, step)
            part = source.at[rows] if layer is None else source.at[layer, rows]
            units.append([copy(part, target.at[pl.ds(j * step, step)])])
    ahead = AHEAD if load_p else len(units)
    begun, ended = [0], [0]

    def begin():
        while begun[0] < min(ended[0] + ahead, len(units)):
            for c in units[begun[0]]:
                c.start()
            begun[0] += 1

    def arrive():
        begin()
        for c in units[ended[0]]:
            c.wait()
        ended[0] += 1
        begin()

    begin()

    def put(d, n):
        at = pl.ds(n * tile, tile)
        for c in range(count):
            send[c, :, at] = d[c * half : (c + 1) * half].astype(send.dtype)
            keep[c, :, at] = d[(count + c) * half : (count + c + 1) * half]

    def step(n):
        put(contract_last(x[...], held[n // per][pl.ds(n % per * tile, tile), :]), n)

    first = 0
    if load_x or load_p:
        for j in range(PIECES):
            arrive()

            @pl.when(place >= 0)
            def _(j=j):
                columns = pl.ds(j * piece, piece)
                d = contract_last(x[:, columns], held[0][pl.ds(0, tile), columns])
                if j > 0:
                    d = acc[...] + d
                if j < PIECES - 1:
                    acc[...] = d
                else:
                    put(d, 0)

        first = 1
    for n in range(first, tiles):
        if load_p:
            arrive()

        @pl.when(place >= 0)
        def _(n=n):
            step(n)

    while ended[0] < len(units):
        arrive()


def partial_sums(solved, x, panel, block, orders, place, group, following, half, chips, extras):
    load_x, load_p = x is None, not isinstance(panel, list)
    panels = [in_hbm(panel)] if load_p else panel
    depth = solved.shape[1]
    width = panel.shape[1] if load_p else sum(part.shape[0] for part in panel)
    count = len(group)
    rows = 2 * count * half
    tile = tile_of(width // 2, 256)
    hbm, vmem = pl.BlockSpec(memory_space=pltpu.HBM), pl.BlockSpec(memory_space=pltpu.VMEM)
    operands = [place, in_hbm(solved)]
    in_specs = [pl.BlockSpec(memory_space=pltpu.SMEM), hbm]
    if not load_x:
        operands.append(x)
        in_specs.append(vmem)
    operands += panels
    in_specs += [hbm if load_p else vmem] * len(panels)
    operands += orders
    in_specs += [pl.BlockSpec(memory_space=pl.ANY)] * len(orders)
    operands += [in_hbm(array) for array, *_ in extras]
    in_specs += [hbm] * len(extras)
    shapes = [
        jax.ShapeDtypeStruct((count, half, width), BF16),
        jax.ShapeDtypeStruct((count, half, width), F32),
    ]
    if load_p:
        shapes.append(jax.ShapeDtypeStruct((width, depth), panel.dtype))
    if following:
        shapes.append(jax.ShapeDtypeStruct((2 * len(following) * half, depth), solved.dtype))
    shapes += [
        jax.ShapeDtypeStruct((size, array.shape[-1]), array.dtype) for array, _, _, size in extras
    ]
    scratch = [pltpu.VMEM((rows, depth), solved.dtype)] if load_x else []
    scratch.append(pltpu.VMEM((rows, tile), F32))
    copies = PIECES * (2 * count + 1) + width // tile + 2 * len(following) + PIECES * len(extras)
    scratch.append(pltpu.SemaphoreType.DMA((copies,)))
    cfg = (
        block, half, tile, load_p, load_x, tuple(group), tuple(following), len(orders),
        len(panels), tuple((layer, low) for _, layer, low, _ in extras), chips,
    )
    out = pl.pallas_call(
        functools.partial(partial_kernel, cfg),
        in_specs=in_specs,
        out_specs=[vmem] * len(shapes),
        out_shape=shapes,
        scratch_shapes=scratch,
        compiler_params=pltpu.CompilerParams(vmem_limit_bytes=LIMIT),
        cost_estimate=pl.CostEstimate(
            flops=2 * rows * width * depth,
            bytes_accessed=2 * depth * (rows + width),
            transcendentals=0,
        ),
    )(*operands)
    out = list(out)
    send, keep = out.pop(0), out.pop(0)
    held = [out.pop(0)] if load_p else panel
    return send, keep, held, out.pop(0) if following else None, out


def residual(b, rhs_ref, parts):
    total = parts[0][...].astype(F32)
    for part in parts[1:]:
        total += part[...].astype(F32)
    return rhs_ref[:, b, :].astype(F32) - total


def blocks_of(mine, members, width):
    return [
        pl.ds(pl.multiple_of((mine ^ offset) * width, width), width)
        for offset in range(members)
    ]


def solve_first_kernel(count, cols, place, rhs, *refs):
    parts, inverse, outs = refs[:count], refs[count], refs[count + 1 :]
    members, width = len(outs), rhs.shape[2]
    at = blocks_of(place[0] // cols, members, width)
    res = residual(0, rhs, parts).astype(BF16)
    for offset in range(members - 1, -1, -1):
        d = jnp.dot(res, inverse[:, at[offset]], preferred_element_type=F32)
        outs[offset][...] = d.astype(outs[offset].dtype)


def carry(firsts, link, at, offsets):
    total = None
    for first, offset in zip(firsts, offsets):
        d = contract_last(first[...], link[:, at[offset]])
        total = d if total is None else total + d
    return total


def carry_kernel(members, offsets, cols, place, *refs):
    firsts, link, out = refs[:-2], refs[-2], refs[-1]
    at = blocks_of(place[0] // cols, members, out.shape[1])
    out[...] = carry(firsts, link, at, offsets)


def solve_second_kernel(count, members, offsets, cols, place, rhs, *refs):
    parts, refs = refs[:count], refs[count:]
    early, refs = refs[0], refs[1:]
    firsts, refs = refs[: len(offsets)], refs[len(offsets) :]
    link, inverse, outs = refs[0], refs[1], refs[2:]
    at = blocks_of(place[0] // cols, members, rhs.shape[2])
    carried = early[...]
    if offsets:
        carried += carry(firsts, link, at, offsets)
    res = (residual(1, rhs, parts) - carried).astype(BF16)
    for offset in range(members - 1, -1, -1):
        d = jnp.dot(res, inverse[:, at[offset]], preferred_element_type=F32)
        outs[offset][...] = d.astype(outs[offset].dtype)


def solve(kernel, flops, place, rhs, parts, rest, members):
    half, _, width = rhs.shape
    vmem = pl.BlockSpec(memory_space=pltpu.VMEM)
    shapes = [
        jax.ShapeDtypeStruct((half, width), BF16 if offset else F32) for offset in range(members)
    ]
    return pl.pallas_call(
        kernel,
        in_specs=[pl.BlockSpec(memory_space=pltpu.SMEM)] + [vmem] * (1 + len(parts) + len(rest)),
        out_specs=[vmem] * members,
        out_shape=shapes,
        compiler_params=pltpu.CompilerParams(vmem_limit_bytes=LIMIT),
        cost_estimate=pl.CostEstimate(flops=flops, bytes_accessed=flops // half, transcendentals=0),
    )(place, rhs, *parts, *rest)


def result_kernel(first, *refs):
    parts, out = refs[:-1], refs[-1]
    total = parts[0][...].astype(F32)
    for part in parts[1:]:
        total += part[...].astype(F32)
    out[:, 0, :] = first[...]
    out[:, 1, :] = total.astype(BF16)


def plan_of(chips):
    plan = [(0, [o]) for o in range(chips - 1, -1, -1)]
    return plan + [(1, [o + 1, o] if chips > 1 else [o]) for o in range(max(chips - 2, 0), -1, -2)]


def local(members, chips, rhs, solved, panel, inverse, link):
    half, _, width = rhs.shape
    cols = 2 * chips
    place = lax.axis_index(("row", "col")).astype(jnp.int32)[None]

    def across_row(value, offset):
        return lax.ppermute(value, "row", [(i, i ^ offset) for i in range(members)])

    def across_col(value, offset):
        return lax.ppermute(value, "col", [(i, i ^ offset) for i in range(cols)])

    plan = plan_of(chips)
    last = len(plan) - 1

    extras = [[] for _ in plan]
    extras[chips].append(("inverse", inverse, 0, 0, width))
    piece = width // 2
    extras[max(0, chips - 2)].append(("low", panel, 1, 0, piece))
    extras[chips - 1].append(("high", panel, 1, piece, piece))
    extras[last].append(("link", link, None, 0, width))
    extras[last].append(("second", inverse, 1, 0, width))

    flops = 2 * half * width * width * members
    sums, kept, passing = [[], []], {}, {}
    due = [[] for _ in plan]
    x, held = None, panel
    for n, (b, group) in enumerate(plan):
        if b == 1 and plan[n - 1][0] == 0:
            held = [kept["low"], kept["high"]]
        following = plan[n + 1][1] if n < last else []
        orders = due[n]
        if n == last:
            parts = solve(
                functools.partial(solve_first_kernel, len(sums[0]), cols),
                flops, place, rhs, sums[0], [kept["inverse"]], members,
            )
            orders = due[n] + [parts[members > 1]]
        send, keep, held, x, got = partial_sums(
            solved, x, held, b, orders, place,
            group, following, half, chips, [e[1:] for e in extras[n]],
        )
        kept.update(zip([e[0] for e in extras[n]], got))
        other = across_col(send, 1)
        for at, offset in enumerate(group):
            pair = keep[at], other[at]
            if offset == 0:
                sums[b] += pair
                continue
            value = pair[0] + pair[1].astype(F32)
            if offset % 2 == 0:
                value += passing.pop((b, offset)).astype(F32)
            value = value.astype(BF16)
            due[min(last, n + (2 if offset % 2 else 3))].append(value)
            arrived = across_col(value, 2 if offset % 2 else 2 * offset)
            if offset > 1 and offset % 2:
                passing[b, offset - 1] = arrived
            else:
                sums[b].append(arrived)

    total = parts[0]
    for offset in range(1, members):
        total += across_row(parts[offset], offset).astype(F32)
    first = total.astype(BF16)
    firsts = [first] + [across_row(first, o) for o in range(1, members)]
    early = sorted({0, members // 2 if members > 2 else 0})
    late = [o for o in range(members) if o not in early]
    vmem = pl.BlockSpec(memory_space=pltpu.VMEM)
    carried = pl.pallas_call(
        functools.partial(carry_kernel, members, early, cols),
        in_specs=[pl.BlockSpec(memory_space=pltpu.SMEM)] + [vmem] * (1 + len(early)),
        out_specs=vmem,
        out_shape=jax.ShapeDtypeStruct((half, width), F32),
        name="carry",
        compiler_params=pltpu.CompilerParams(vmem_limit_bytes=LIMIT),
        cost_estimate=pl.CostEstimate(
            flops=2 * half * width * width, bytes_accessed=width * width, transcendentals=0
        ),
    )(place, *[firsts[o] for o in early], kept["link"])
    parts = solve(
        functools.partial(solve_second_kernel, len(sums[1]), members, late, cols),
        2 * flops, place, rhs, sums[1],
        [carried] + [firsts[o] for o in late] + [kept["link"], kept["second"]], members,
    )
    arrived = [across_row(parts[offset], offset) for offset in range(1, members)]
    return pl.pallas_call(
        result_kernel,
        out_shape=jax.ShapeDtypeStruct(rhs.shape, rhs.dtype),
        name="result",
        compiler_params=pltpu.CompilerParams(vmem_limit_bytes=LIMIT),
    )(first, parts[0], *arrived)


def solution(mesh):
    members, chips = mesh.shape["row"], mesh.shape["col"] // 2

    def body(*arrays):
        return local(members, chips, *arrays)

    return jax.shard_map(
        body,
        mesh=mesh,
        in_specs=(
            P("col", None, "row"),
            P(None, "col"),
            P(None, "row", "col"),
            P(None, "row", None),
            P("row", None),
        ),
        out_specs=P("col", None, "row"),
        check_vma=False,
    )
```

```python
import functools

import jax
import jax.numpy as jnp
from jax import lax
from jax.experimental import pallas as pl
from jax.experimental.pallas import tpu as pltpu
from jax.sharding import PartitionSpec as P


F32, BF16 = jnp.float32, jnp.bfloat16
AHEAD = 3
PIECES = 4
LIMIT = 8 << 20


def contract_last(a, b):
    return lax.dot_general(a, b, (((1,), (1,)), ((), ())), preferred_element_type=F32)


def tile_of(size, most):
    while size % most:
        most //= 2
    return most


def in_hbm(array):
    return pltpu.with_memory_space_constraint(array, pltpu.HBM)


def partial_kernel(cfg, *refs):
    block, low_row, half, tile, load_p, load_x, group, following, ordered, blocks, extras, chips = cfg
    refs = list(refs)
    place, solved = refs.pop(0)[0], refs.pop(0)
    x = None if load_x else refs.pop(0)
    held = [refs.pop(0) for _ in range(blocks)]
    panel = held[0]
    for _ in range(ordered):
        refs.pop(0)
    wanted = [refs.pop(0) for _ in extras]
    send, keep = refs.pop(0), refs.pop(0)
    if load_p:
        held = [refs.pop(0)]
    if load_x:
        x = refs.pop(0)
    upcoming = refs.pop(0) if following else None
    fetched = [refs.pop(0) for _ in extras]
    acc, sems = refs
    depth = solved.shape[1]
    piece = depth // PIECES
    per = held[0].shape[0] // tile
    tiles = per * len(held)
    count = len(group)
    chip, core = lax.rem(place, 2 * chips) // 2, lax.rem(place, 2)
    used = [0]

    def copy(source, target):
        used[0] += 1
        return pltpu.make_async_copy(source, target, sems.at[used[0] - 1])

    def rows_copy(offsets, target, at, columns):
        parity = 1 - core if at < len(offsets) else core
        start = ((chip ^ offsets[at % len(offsets)]) * 2 + parity) * half
        return copy(
            solved.at[pl.ds(pl.multiple_of(start, half), half), columns],
            target.at[pl.ds(at * half, half), columns],
        )

    def panel_copy(n, columns):
        rows = pl.ds(n * tile, tile)
        return copy(panel.at[block, pl.ds(low_row + n * tile, tile), columns], held[0].at[rows, columns])

    units = []
    if load_x or load_p:
        for j in range(PIECES):
            columns = pl.ds(j * piece, piece)
            unit = [rows_copy(group, x, s, columns) for s in range(2 * count)] if load_x else []
            units.append(unit + ([panel_copy(0, columns)] if load_p else []))
    if load_p:
        units += [[panel_copy(n, slice(None))] for n in range(1, tiles)]
    units += [[rows_copy(following, upcoming, s, slice(None))] for s in range(2 * len(following))]
    for (layer, low), source, target in zip(extras, wanted, fetched):
        step = target.shape[0] // PIECES
        for j in range(PIECES):
            rows = pl.ds(low + j * step, step)
            part = source.at[rows] if layer is None else source.at[layer, rows]
            units.append([copy(part, target.at[pl.ds(j * step, step)])])
    ahead = AHEAD if load_p else len(units)
    begun, ended = [0], [0]

    def begin():
        while begun[0] < min(ended[0] + ahead, len(units)):
            for c in units[begun[0]]:
                c.start()
            begun[0] += 1

    def arrive():
        begin()
        for c in units[ended[0]]:
            c.wait()
        ended[0] += 1
        begin()

    begin()

    def put(d, n):
        at = pl.ds(n * tile, tile)
        for c in range(count):
            send[c, :, at] = d[c * half : (c + 1) * half].astype(send.dtype)
            keep[c, :, at] = d[(count + c) * half : (count + c + 1) * half]

    def step(n):
        put(contract_last(x[...], held[n // per][pl.ds(n % per * tile, tile), :]), n)

    first = 0
    if load_x or load_p:
        for j in range(PIECES):
            arrive()

            @pl.when(place >= 0)
            def _(j=j):
                columns = pl.ds(j * piece, piece)
                d = contract_last(x[:, columns], held[0][pl.ds(0, tile), columns])
                if j > 0:
                    d = acc[...] + d
                if j < PIECES - 1:
                    acc[...] = d
                else:
                    put(d, 0)

        first = 1
    for n in range(first, tiles):
        if load_p:
            arrive()

        @pl.when(place >= 0)
        def _(n=n):
            step(n)

    while ended[0] < len(units):
        arrive()


def partial_sums(solved, x, panel, span, orders, place, group, following, half, chips, extras):
    load_x, load_p = x is None, not isinstance(panel, list)
    panels = [in_hbm(panel)] if load_p else panel
    depth = solved.shape[1]
    block, low_row, width = span if load_p else (0, 0, sum(part.shape[0] for part in panel))
    count = len(group)
    rows = 2 * count * half
    tile = tile_of(width if load_p else panels[0].shape[0], 256)
    hbm, vmem = pl.BlockSpec(memory_space=pltpu.HBM), pl.BlockSpec(memory_space=pltpu.VMEM)
    operands = [place, in_hbm(solved)]
    in_specs = [pl.BlockSpec(memory_space=pltpu.SMEM), hbm]
    if not load_x:
        operands.append(x)
        in_specs.append(vmem)
    operands += panels
    in_specs += [hbm if load_p else vmem] * len(panels)
    operands += orders
    in_specs += [pl.BlockSpec(memory_space=pl.ANY)] * len(orders)
    operands += [in_hbm(array) for array, *_ in extras]
    in_specs += [hbm] * len(extras)
    shapes = [
        jax.ShapeDtypeStruct((count, half, width), BF16),
        jax.ShapeDtypeStruct((count, half, width), F32),
    ]
    if load_p:
        shapes.append(jax.ShapeDtypeStruct((width, depth), panel.dtype))
    if load_x:
        shapes.append(jax.ShapeDtypeStruct((rows, depth), solved.dtype))
    if following:
        shapes.append(jax.ShapeDtypeStruct((2 * len(following) * half, depth), solved.dtype))
    shapes += [
        jax.ShapeDtypeStruct((size, array.shape[-1]), array.dtype) for array, _, _, size in extras
    ]
    scratch = [pltpu.VMEM((rows, tile), F32)]
    copies = PIECES * (2 * count + 1) + width // tile + 2 * len(following) + PIECES * len(extras)
    scratch.append(pltpu.SemaphoreType.DMA((copies,)))
    cfg = (
        block, low_row, half, tile, load_p, load_x, tuple(group), tuple(following), len(orders),
        len(panels), tuple((layer, low) for _, layer, low, _ in extras), chips,
    )
    out = pl.pallas_call(
        functools.partial(partial_kernel, cfg),
        in_specs=in_specs,
        out_specs=[vmem] * len(shapes),
        out_shape=shapes,
        scratch_shapes=scratch,
        compiler_params=pltpu.CompilerParams(vmem_limit_bytes=LIMIT),
        cost_estimate=pl.CostEstimate(
            flops=2 * rows * width * depth,
            bytes_accessed=2 * depth * (rows + width),
            transcendentals=0,
        ),
    )(*operands)
    out = list(out)
    send, keep = out.pop(0), out.pop(0)
    held = [out.pop(0)] if load_p else []
    if load_x:
        x = out.pop(0)
    return send, keep, held, out.pop(0) if following else x, out


def residual(b, rhs_ref, parts, counts):
    total, parts = rhs_ref[:, b, :].astype(F32), list(parts)
    for count in counts:
        pieces = [parts.pop(0)[...].astype(F32) for _ in range(count)]
        total -= pieces[0] if count == 1 else jnp.concatenate(pieces, axis=1)
    return total


def blocks_of(mine, members, width):
    return [
        pl.ds(pl.multiple_of((mine ^ offset) * width, width), width)
        for offset in range(members)
    ]


def solve_first_kernel(counts, cols, place, rhs, *refs):
    count = sum(counts)
    parts, inverse, outs = refs[:count], refs[count], refs[count + 1 :]
    members, width = len(outs), rhs.shape[2]
    at = blocks_of(place[0] // cols, members, width)
    res = residual(0, rhs, parts, counts).astype(BF16)
    for offset in range(members - 1, -1, -1):
        d = jnp.dot(res, inverse[:, at[offset]], preferred_element_type=F32)
        outs[offset][...] = d.astype(outs[offset].dtype)


def carry(firsts, link, at, offsets):
    total = None
    for first, offset in zip(firsts, offsets):
        d = contract_last(first[...], link[:, at[offset]])
        total = d if total is None else total + d
    return total


def carry_kernel(members, offsets, cols, place, *refs):
    firsts, link, out = refs[:-2], refs[-2], refs[-1]
    at = blocks_of(place[0] // cols, members, out.shape[1])
    out[...] = carry(firsts, link, at, offsets)


def solve_second_kernel(counts, members, offsets, cols, place, rhs, *refs):
    count = sum(counts)
    parts, refs = refs[:count], refs[count:]
    early, refs = refs[0], refs[1:]
    firsts, refs = refs[: len(offsets)], refs[len(offsets) :]
    link, inverse, outs = refs[0], refs[1], refs[2:]
    at = blocks_of(place[0] // cols, members, rhs.shape[2])
    carried = early[...]
    if offsets:
        carried += carry(firsts, link, at, offsets)
    res = (residual(1, rhs, parts, counts) - carried).astype(BF16)
    for offset in range(members - 1, -1, -1):
        d = jnp.dot(res, inverse[:, at[offset]], preferred_element_type=F32)
        outs[offset][...] = d.astype(outs[offset].dtype)


def solve(kernel, flops, place, rhs, parts, rest, members):
    half, _, width = rhs.shape
    vmem = pl.BlockSpec(memory_space=pltpu.VMEM)
    shapes = [
        jax.ShapeDtypeStruct((half, width), BF16 if offset else F32) for offset in range(members)
    ]
    return pl.pallas_call(
        kernel,
        in_specs=[pl.BlockSpec(memory_space=pltpu.SMEM)] + [vmem] * (1 + len(parts) + len(rest)),
        out_specs=[vmem] * members,
        out_shape=shapes,
        compiler_params=pltpu.CompilerParams(vmem_limit_bytes=LIMIT),
        cost_estimate=pl.CostEstimate(flops=flops, bytes_accessed=flops // half, transcendentals=0),
    )(place, rhs, *parts, *rest)


def result_kernel(first, *refs):
    parts, out = refs[:-1], refs[-1]
    total = parts[0][...].astype(F32)
    for part in parts[1:]:
        total += part[...].astype(F32)
    out[:, 0, :] = first[...]
    out[:, 1, :] = total.astype(BF16)


def plan_of(chips):
    far = list(range(chips - 1, max(chips - 3, -1), -1))
    plan = [(0, far, 0), (0, far, 1)]
    plan += [(0, [o], None) for o in range(far[-1] - 1, -1, -1)]
    pairs = [[o + 1, o] if chips > 1 else [o] for o in range(max(chips - 2, 0), -1, -2)]
    return plan + [(1, pair, None) for pair in pairs]


def local(members, chips, rhs, solved, panel, inverse, link):
    half, _, width = rhs.shape
    cols = 2 * chips
    place = lax.axis_index(("row", "col")).astype(jnp.int32)[None]

    def across_row(value, offset):
        return lax.ppermute(value, "row", [(i, i ^ offset) for i in range(members)])

    def across_col(value, offset):
        return lax.ppermute(value, "col", [(i, i ^ offset) for i in range(cols)])

    plan = plan_of(chips)
    last = len(plan) - 1

    extras = [[] for _ in plan]
    ahead = [n for n, (b, _, _) in enumerate(plan) if b == 0]
    extras[min(len(ahead), last - 1)].append(("inverse", inverse, 0, 0, width))
    piece = width // 2
    extras[ahead[-2]].append(("low", panel, 1, 0, piece))
    extras[ahead[-1]].append(("high", panel, 1, piece, piece))
    extras[last].append(("link", link, None, 0, width))
    extras[last].append(("second", inverse, 1, 0, width))

    flops = 2 * half * width * width * members
    kept, passing = {}, {}
    sums = [{}, {}]
    due = [[] for _ in plan]

    def term(b, key, value):
        sums[b].setdefault(key, []).append(value)

    def counts(b):
        return tuple(len(pieces) for pieces in sums[b].values())

    def flat(b):
        return [value for pieces in sums[b].values() for value in pieces]

    x, blocks = None, []
    for n, (b, group, part) in enumerate(plan):
        if n == len(ahead):
            blocks = [kept["low"], kept["high"]]
        follows = n < last and plan[n + 1][1] != group
        following = plan[n + 1][1] if follows else []
        orders = due[n]
        if n == last:
            parts = solve(
                functools.partial(solve_first_kernel, counts(0), cols),
                flops, place, rhs, flat(0), [kept["inverse"]], members,
            )
            orders = due[n] + [parts[members > 1]]
        span = None if part is None else (b, part * piece, piece)
        send, keep, held, x, got = partial_sums(
            solved, x, blocks if part is None else panel, span, orders, place,
            group, following, half, chips, [e[1:] for e in extras[n]],
        )
        blocks = blocks + held
        kept.update(zip([e[0] for e in extras[n]], got))
        other = across_col(send, 1)
        for at, offset in enumerate(group):
            if offset == 0:
                term(b, "own", keep[at])
                term(b, "swap", other[at])
                continue
            value = keep[at] + other[at].astype(F32)
            if offset % 2 == 0:
                value += passing.pop((b, offset, part)).astype(F32)
            value = value.astype(BF16)
            due[min(last, n + (2 if offset % 2 else 3))].append(value)
            arrived = across_col(value, 2 if offset % 2 else 2 * offset)
            if offset > 1 and offset % 2:
                passing[b, offset - 1, part] = arrived
            else:
                term(b, offset, arrived)

    total = parts[0]
    for offset in range(1, members):
        total += across_row(parts[offset], offset).astype(F32)
    first = total.astype(BF16)
    firsts = [first] + [across_row(first, o) for o in range(1, members)]
    early = sorted({0, members // 2 if members > 2 else 0})
    late = [o for o in range(members) if o not in early]
    vmem = pl.BlockSpec(memory_space=pltpu.VMEM)
    carried = pl.pallas_call(
        functools.partial(carry_kernel, members, early, cols),
        in_specs=[pl.BlockSpec(memory_space=pltpu.SMEM)] + [vmem] * (1 + len(early)),
        out_specs=vmem,
        out_shape=jax.ShapeDtypeStruct((half, width), F32),
        name="carry",
        compiler_params=pltpu.CompilerParams(vmem_limit_bytes=LIMIT),
        cost_estimate=pl.CostEstimate(
            flops=2 * half * width * width, bytes_accessed=width * width, transcendentals=0
        ),
    )(place, *[firsts[o] for o in early], kept["link"])
    parts = solve(
        functools.partial(solve_second_kernel, counts(1), members, late, cols),
        2 * flops, place, rhs, flat(1),
        [carried] + [firsts[o] for o in late] + [kept["link"], kept["second"]], members,
    )
    arrived = [across_row(parts[offset], offset) for offset in range(1, members)]
    return pl.pallas_call(
        result_kernel,
        out_shape=jax.ShapeDtypeStruct(rhs.shape, rhs.dtype),
        name="result",
        compiler_params=pltpu.CompilerParams(vmem_limit_bytes=LIMIT),
    )(first, parts[0], *arrived)


def solution(mesh):
    members, chips = mesh.shape["row"], mesh.shape["col"] // 2

    def body(*arrays):
        return local(members, chips, *arrays)

    return jax.shard_map(
        body,
        mesh=mesh,
        in_specs=(
            P("col", None, "row"),
            P(None, "col"),
            P(None, "row", "col"),
            P(None, "row", None),
            P("row", None),
        ),
        out_specs=P("col", None, "row"),
        check_vma=False,
    )
```

```python
import functools

import jax
import jax.numpy as jnp
from jax import lax
from jax.experimental import pallas as pl
from jax.experimental.pallas import tpu as pltpu
from jax.sharding import PartitionSpec as P


F32, BF16 = jnp.float32, jnp.bfloat16
AHEAD = 3
PIECES = 4
LIMIT = 6 << 20


def contract_last(a, b):
    return lax.dot_general(a, b, (((1,), (1,)), ((), ())), preferred_element_type=F32)


def tile_of(size, most):
    while size % most:
        most //= 2
    return most


def in_hbm(array):
    return pltpu.with_memory_space_constraint(array, pltpu.HBM)


def partial_kernel(cfg, *refs):
    block, low_row, half, tile, load_p, load_x, group, following, ordered, blocks, within, extras, chips = cfg
    refs = list(refs)
    place, solved = refs.pop(0)[0], refs.pop(0)
    x = None if load_x else refs.pop(0)
    held = [refs.pop(0) for _ in range(blocks)]
    panel = held[0]
    for _ in range(ordered):
        refs.pop(0)
    wanted = [refs.pop(0) for _ in extras]
    send, keep = refs.pop(0), refs.pop(0)
    if load_p:
        held = [refs.pop(0)]
    if load_x:
        x = refs.pop(0)
    upcoming = refs.pop(0) if following else None
    fetched = [refs.pop(0) for _ in extras]
    acc, sems = refs
    depth = solved.shape[1]
    piece = depth // PIECES
    per = held[0].shape[0] // tile
    tiles = per * len(held)
    begin_tile, end_tile = [tiles * edge // within[1] for edge in (within[0], within[0] + 1)]
    count = len(group)
    chip, core = lax.rem(place, 2 * chips) // 2, lax.rem(place, 2)
    used = [0]

    def copy(source, target):
        used[0] += 1
        return pltpu.make_async_copy(source, target, sems.at[used[0] - 1])

    def rows_copy(offsets, target, at, columns):
        parity = 1 - core if at < len(offsets) else core
        start = ((chip ^ offsets[at % len(offsets)]) * 2 + parity) * half
        return copy(
            solved.at[pl.ds(pl.multiple_of(start, half), half), columns],
            target.at[pl.ds(at * half, half), columns],
        )

    def panel_copy(n, columns):
        rows = pl.ds(n * tile, tile)
        return copy(panel.at[block, pl.ds(low_row + n * tile, tile), columns], held[0].at[rows, columns])

    units = []
    if load_x or load_p:
        for j in range(PIECES):
            columns = pl.ds(j * piece, piece)
            unit = [rows_copy(group, x, s, columns) for s in range(2 * count)] if load_x else []
            units.append(unit + ([panel_copy(0, columns)] if load_p else []))
    if load_p:
        units += [[panel_copy(n, slice(None))] for n in range(1, tiles)]
    units += [[rows_copy(following, upcoming, s, slice(None))] for s in range(2 * len(following))]
    for (layer, low), source, target in zip(extras, wanted, fetched):
        step = target.shape[0] // PIECES
        for j in range(PIECES):
            rows = pl.ds(low + j * step, step)
            part = source.at[rows] if layer is None else source.at[layer, rows]
            units.append([copy(part, target.at[pl.ds(j * step, step)])])
    ahead = AHEAD if load_p else len(units)
    begun, ended = [0], [0]

    def begin():
        while begun[0] < min(ended[0] + ahead, len(units)):
            for c in units[begun[0]]:
                c.start()
            begun[0] += 1

    def arrive():
        begin()
        for c in units[ended[0]]:
            c.wait()
        ended[0] += 1
        begin()

    begin()

    def put(d, n):
        at = pl.ds((n - begin_tile) * tile, tile)
        for c in range(count):
            send[c, :, at] = d[c * half : (c + 1) * half].astype(send.dtype)
            keep[c, :, at] = d[(count + c) * half : (count + c + 1) * half]

    def step(n):
        put(contract_last(x[...], held[n // per][pl.ds(n % per * tile, tile), :]), n)

    first = begin_tile
    if load_x or load_p:
        for j in range(PIECES):
            arrive()

            @pl.when(place >= 0)
            def _(j=j):
                columns = pl.ds(j * piece, piece)
                d = contract_last(x[:, columns], held[0][pl.ds(0, tile), columns])
                if j > 0:
                    d = acc[...] + d
                if j < PIECES - 1:
                    acc[...] = d
                else:
                    put(d, 0)

        first = 1
    for n in range(first, end_tile):
        if load_p:
            arrive()

        @pl.when(place >= 0)
        def _(n=n):
            step(n)

    while ended[0] < len(units):
        arrive()


def partial_sums(solved, x, panel, span, orders, place, group, following, half, chips, within, extras):
    load_x, load_p = x is None, not isinstance(panel, list)
    panels = [in_hbm(panel)] if load_p else panel
    depth = solved.shape[1]
    block, low_row, width = span if load_p else (0, 0, sum(part.shape[0] for part in panel))
    count = len(group)
    rows = 2 * count * half
    tile = tile_of(width if load_p else panels[0].shape[0], 256)
    width = width // within[1]
    hbm, vmem = pl.BlockSpec(memory_space=pltpu.HBM), pl.BlockSpec(memory_space=pltpu.VMEM)
    operands = [place, in_hbm(solved)]
    in_specs = [pl.BlockSpec(memory_space=pltpu.SMEM), hbm]
    if not load_x:
        operands.append(x)
        in_specs.append(vmem)
    operands += panels
    in_specs += [hbm if load_p else vmem] * len(panels)
    operands += orders
    in_specs += [pl.BlockSpec(memory_space=pl.ANY)] * len(orders)
    operands += [in_hbm(array) for array, *_ in extras]
    in_specs += [hbm] * len(extras)
    shapes = [
        jax.ShapeDtypeStruct((count, half, width), BF16),
        jax.ShapeDtypeStruct((count, half, width), F32),
    ]
    if load_p:
        shapes.append(jax.ShapeDtypeStruct((span[2], depth), panel.dtype))
    if load_x:
        shapes.append(jax.ShapeDtypeStruct((rows, depth), solved.dtype))
    if following:
        shapes.append(jax.ShapeDtypeStruct((2 * len(following) * half, depth), solved.dtype))
    shapes += [
        jax.ShapeDtypeStruct((size, array.shape[-1]), array.dtype) for array, _, _, size in extras
    ]
    scratch = [pltpu.VMEM((rows, tile), F32)]
    copies = PIECES * (2 * count + 1) + panels[0].shape[-2] // tile + 2 * len(following) + PIECES * len(extras)
    scratch.append(pltpu.SemaphoreType.DMA((copies,)))
    cfg = (
        block, low_row, half, tile, load_p, load_x, tuple(group), tuple(following), len(orders),
        len(panels), within, tuple((layer, low) for _, layer, low, _ in extras), chips,
    )
    out = pl.pallas_call(
        functools.partial(partial_kernel, cfg),
        in_specs=in_specs,
        out_specs=[vmem] * len(shapes),
        out_shape=shapes,
        scratch_shapes=scratch,
        compiler_params=pltpu.CompilerParams(vmem_limit_bytes=LIMIT),
        cost_estimate=pl.CostEstimate(
            flops=2 * rows * width * depth,
            bytes_accessed=2 * depth * (rows + width),
            transcendentals=0,
        ),
    )(*operands)
    out = list(out)
    send, keep = out.pop(0), out.pop(0)
    held = [out.pop(0)] if load_p else []
    if load_x:
        x = out.pop(0)
    return send, keep, held, out.pop(0) if following else x, out


def residual(b, rhs_ref, parts, counts):
    total, parts = rhs_ref[:, b, :].astype(F32), list(parts)
    for count in counts:
        pieces = [parts.pop(0)[...].astype(F32) for _ in range(count)]
        total -= pieces[0] if count == 1 else jnp.concatenate(pieces, axis=1)
    return total


def blocks_of(mine, members, width):
    return [
        pl.ds(pl.multiple_of((mine ^ offset) * width, width), width)
        for offset in range(members)
    ]


def solve_first_kernel(counts, cols, place, rhs, *refs):
    count = sum(counts)
    parts, inverse, outs = refs[:count], refs[count], refs[count + 1 :]
    members, width = len(outs), rhs.shape[2]
    at = blocks_of(place[0] // cols, members, width)
    res = residual(0, rhs, parts, counts).astype(BF16)
    for offset in range(members - 1, -1, -1):
        d = jnp.dot(res, inverse[:, at[offset]], preferred_element_type=F32)
        outs[offset][...] = d.astype(outs[offset].dtype)


def carry(firsts, link, at, offsets):
    total = None
    for first, offset in zip(firsts, offsets):
        d = contract_last(first[...], link[:, at[offset]])
        total = d if total is None else total + d
    return total


def carry_kernel(members, offsets, cols, place, *refs):
    firsts, link, out = refs[:-3], refs[-3], refs[-1]
    at = blocks_of(place[0] // cols, members, out.shape[1])
    out[...] = carry(firsts, link, at, offsets)


def solve_second_kernel(counts, members, offsets, cols, place, rhs, *refs):
    count = sum(counts)
    parts, refs = refs[:count], refs[count:]
    early, refs = refs[0], refs[1:]
    firsts, refs = refs[: len(offsets)], refs[len(offsets) :]
    link, inverse, outs = refs[0], refs[1], refs[2:]
    at = blocks_of(place[0] // cols, members, rhs.shape[2])
    carried = early[...]
    if offsets:
        carried += carry(firsts, link, at, offsets)
    out, res = outs
    value = (residual(1, rhs, parts, counts) - carried).astype(BF16)
    res[...] = value
    d = jnp.dot(value, inverse[:, at[members - 1]], preferred_element_type=F32)
    out[...] = d.astype(out.dtype)


def second_rest_kernel(members, cols, place, res, inverse, *outs):
    at = blocks_of(place[0] // cols, members, res.shape[1])
    for offset in range(members - 2, -1, -1):
        d = jnp.dot(res[...], inverse[:, at[offset]], preferred_element_type=F32)
        outs[offset][...] = d.astype(outs[offset].dtype)


def solve(kernel, flops, place, operands, shape, types):
    vmem = pl.BlockSpec(memory_space=pltpu.VMEM)
    return pl.pallas_call(
        kernel,
        in_specs=[pl.BlockSpec(memory_space=pltpu.SMEM)] + [vmem] * len(operands),
        out_specs=[vmem] * len(types),
        out_shape=[jax.ShapeDtypeStruct(shape, kind) for kind in types],
        compiler_params=pltpu.CompilerParams(vmem_limit_bytes=LIMIT),
        cost_estimate=pl.CostEstimate(
            flops=flops, bytes_accessed=flops // shape[0], transcendentals=0
        ),
    )(place, *operands)


def result_kernel(first, *refs):
    parts, out = refs[:-1], refs[-1]
    total = parts[0][...].astype(F32)
    for part in parts[1:]:
        total += part[...].astype(F32)
    out[:, 0, :] = first[...]
    out[:, 1, :] = total.astype(BF16)


def plan_of(chips):
    plan = [(0, [o], (0, 1)) for o in range(chips - 1, 0, -1)]
    plan += [(0, [0], (0, 2)), (0, [0], (1, 2))] if plan else [(0, [0], (0, 1))]
    plan += [(1, [o + 1, o], (0, 1)) for o in range(chips - 2, 0, -2)]
    return plan + [(1, [o], (0, 1)) for o in ([1, 0] if chips > 1 else [0])]


def deadline(plan, n, offset):
    odd, last = offset % 2, len(plan) - 1
    return min(last, n + (1 if plan[n][0] else 2 if odd else 3))


def local(members, chips, rhs, solved, panel, inverse, link):
    half, _, width = rhs.shape
    cols = 2 * chips
    place = lax.axis_index(("row", "col")).astype(jnp.int32)[None]

    def across_row(value, offset):
        return lax.ppermute(value, "row", [(i, i ^ offset) for i in range(members)])

    def across_col(value, offset):
        return lax.ppermute(value, "col", [(i, i ^ offset) for i in range(cols)])

    plan = plan_of(chips)
    last = len(plan) - 1

    extras = [[] for _ in plan]
    ahead = [n for n, (b, _, _) in enumerate(plan) if b == 0]
    extras[len(ahead) if last > len(ahead) + 1 else 0].append(("inverse", inverse, 0, 0, width))
    piece = width // 2
    extras[max(0, ahead[-1] - 3)].append(("low", panel, 1, 0, piece))
    extras[max(0, ahead[-1] - 2)].append(("high", panel, 1, piece, piece))
    extras[last - 1].append(("link", link, None, 0, width))
    extras[last].append(("second", inverse, 1, 0, width))

    flops = 2 * half * width * width * members
    kept, passing = {}, {}
    sums = [{}, {}]
    due = [[] for _ in plan]

    def term(b, key, value):
        sums[b].setdefault(key, []).append(value)

    def counts(b):
        return tuple(len(pieces) for pieces in sums[b].values())

    def flat(b):
        return [value for pieces in sums[b].values() for value in pieces]

    x, blocks = None, []
    for n, (b, group, part) in enumerate(plan):
        if n == len(ahead):
            blocks = [kept["low"], kept["high"]]
        follows = n < last and plan[n + 1][1] != group
        following = plan[n + 1][1] if follows else []
        orders = due[n]
        if n == last - 1:
            parts = solve(
                functools.partial(solve_first_kernel, counts(0), cols),
                flops, place, [rhs, *flat(0), kept["inverse"]],
                (half, width), [F32] + [BF16] * (members - 1),
            )
            orders = due[n] + [parts[members > 1]]
        if n == last:
            total = parts[0]
            for offset in range(1, members):
                total += across_row(parts[offset], offset).astype(F32)
            first = total.astype(BF16)
            orders = due[n] + [first]
        send, keep, held, x, got = partial_sums(
            solved, x, blocks if n else panel, (0, 0, width), orders, place,
            group, following, half, chips, part, [e[1:] for e in extras[n]],
        )
        blocks = blocks + held
        kept.update(zip([e[0] for e in extras[n]], got))
        other = across_col(send, 1)
        for at, offset in enumerate(group):
            if offset == 0:
                term(b, "own", keep[at])
                term(b, "swap", other[at])
                continue
            value = keep[at] + other[at].astype(F32)
            if offset % 2 == 0:
                value += passing.pop((b, offset)).astype(F32)
            value = value.astype(BF16)
            due[deadline(plan, n, offset)].append(value)
            arrived = across_col(value, 2 if offset % 2 else 2 * offset)
            if offset > 1 and offset % 2:
                passing[b, offset - 1] = arrived
            else:
                term(b, offset, arrived)

    firsts = [first] + [across_row(first, o) for o in range(1, members)]
    early = sorted({0, members // 2 if members > 2 else 0})
    late = [o for o in range(members) if o not in early]
    vmem = pl.BlockSpec(memory_space=pltpu.VMEM)
    carried = pl.pallas_call(
        functools.partial(carry_kernel, members, early, cols),
        in_specs=[pl.BlockSpec(memory_space=pltpu.SMEM)] + [vmem] * (1 + len(early))
        + [pl.BlockSpec(memory_space=pl.ANY)],
        out_specs=vmem,
        out_shape=jax.ShapeDtypeStruct((half, width), F32),
        name="carry",
        compiler_params=pltpu.CompilerParams(vmem_limit_bytes=LIMIT),
        cost_estimate=pl.CostEstimate(
            flops=2 * half * width * width, bytes_accessed=width * width, transcendentals=0
        ),
    )(place, *[firsts[o] for o in early], kept["link"], keep)
    shape = (half, width)
    edge, res = solve(
        functools.partial(solve_second_kernel, counts(1), members, late, cols),
        flops, place,
        [rhs, *flat(1), carried, *[firsts[o] for o in late], kept["link"], kept["second"]],
        shape, [BF16, BF16],
    )
    parts = solve(
        functools.partial(second_rest_kernel, members, cols),
        flops, place, [res, kept["second"]], shape, [F32] + [BF16] * (members - 2),
    )
    parts = list(parts) + [edge]
    arrived = [across_row(parts[offset], offset) for offset in range(1, members)]
    return pl.pallas_call(
        result_kernel,
        out_shape=jax.ShapeDtypeStruct(rhs.shape, rhs.dtype),
        name="result",
        compiler_params=pltpu.CompilerParams(vmem_limit_bytes=LIMIT),
    )(first, parts[0], *arrived)


def solution(mesh):
    members, chips = mesh.shape["row"], mesh.shape["col"] // 2

    def body(*arrays):
        return local(members, chips, *arrays)

    return jax.shard_map(
        body,
        mesh=mesh,
        in_specs=(
            P("col", None, "row"),
            P(None, "col"),
            P(None, "row", "col"),
            P(None, "row", None),
            P("row", None),
        ),
        out_specs=P("col", None, "row"),
        check_vma=False,
    )
```

```python
import functools

import jax
import jax.numpy as jnp
from jax import lax
from jax.experimental import pallas as pl
from jax.experimental.pallas import tpu as pltpu
from jax.sharding import PartitionSpec as P


F32, BF16 = jnp.float32, jnp.bfloat16
AHEAD = 3
PIECES = 4
LIMIT = 6 << 20


def contract_last(a, b):
    return lax.dot_general(a, b, (((1,), (1,)), ((), ())), preferred_element_type=F32)


def tile_of(size, most):
    while size % most:
        most //= 2
    return most


def in_hbm(array):
    return pltpu.with_memory_space_constraint(array, pltpu.HBM)


def partial_kernel(cfg, *refs):
    block, low_row, half, tile, load_p, load_x, group, following, ordered, blocks, within, extras, chips = cfg
    refs = list(refs)
    place, solved = refs.pop(0)[0], refs.pop(0)
    x = None if load_x else refs.pop(0)
    held = [refs.pop(0) for _ in range(blocks)]
    panel = held[0]
    for _ in range(ordered):
        refs.pop(0)
    wanted = [refs.pop(0) for _ in extras]
    send, keep = refs.pop(0), refs.pop(0)
    if load_p:
        held = [refs.pop(0)]
    upcoming = refs.pop(0) if following else None
    fetched = [refs.pop(0) for _ in extras]
    if load_x:
        x = refs.pop(0)
    acc, sems = refs
    depth = solved.shape[1]
    piece = depth // PIECES
    per = held[0].shape[0] // tile
    tiles = per * len(held)
    begin_tile, end_tile = [tiles * edge // within[1] for edge in (within[0], within[0] + 1)]
    count = len(group)
    chip, core = lax.rem(place, 2 * chips) // 2, lax.rem(place, 2)
    used = [0]

    def copy(source, target):
        used[0] += 1
        return pltpu.make_async_copy(source, target, sems.at[used[0] - 1])

    def rows_copy(offsets, target, at, columns):
        parity = 1 - core if at < len(offsets) else core
        start = ((chip ^ offsets[at % len(offsets)]) * 2 + parity) * half
        return copy(
            solved.at[pl.ds(pl.multiple_of(start, half), half), columns],
            target.at[pl.ds(at * half, half), columns],
        )

    def panel_copy(n, columns):
        rows = pl.ds(n * tile, tile)
        return copy(panel.at[block, pl.ds(low_row + n * tile, tile), columns], held[0].at[rows, columns])

    units = []
    if load_x or load_p:
        for j in range(PIECES):
            columns = pl.ds(j * piece, piece)
            unit = [rows_copy(group, x, s, columns) for s in range(2 * count)] if load_x else []
            units.append(unit + ([panel_copy(0, columns)] if load_p else []))
    if load_p:
        units += [[panel_copy(n, slice(None))] for n in range(1, tiles)]
    units += [[rows_copy(following, upcoming, s, slice(None))] for s in range(2 * len(following))]
    for (layer, low), source, target in zip(extras, wanted, fetched):
        step = target.shape[0] // PIECES
        for j in range(PIECES):
            rows = pl.ds(low + j * step, step)
            part = source.at[rows] if layer is None else source.at[layer, rows]
            units.append([copy(part, target.at[pl.ds(j * step, step)])])
    ahead = AHEAD if load_p else len(units)
    begun, ended = [0], [0]

    def begin():
        while begun[0] < min(ended[0] + ahead, len(units)):
            for c in units[begun[0]]:
                c.start()
            begun[0] += 1

    def arrive():
        begin()
        for c in units[ended[0]]:
            c.wait()
        ended[0] += 1
        begin()

    begin()

    def put(d, n):
        at = pl.ds((n - begin_tile) * tile, tile)
        for c in range(count):
            send[c, :, at] = d[c * half : (c + 1) * half].astype(send.dtype)
            keep[c, :, at] = d[(count + c) * half : (count + c + 1) * half]

    def step(n):
        put(contract_last(x[...], held[n // per][pl.ds(n % per * tile, tile), :]), n)

    first = begin_tile
    if load_x or load_p:
        for j in range(PIECES):
            arrive()

            @pl.when(place >= 0)
            def _(j=j):
                columns = pl.ds(j * piece, piece)
                d = contract_last(x[:, columns], held[0][pl.ds(0, tile), columns])
                if j > 0:
                    d = acc[...] + d
                if j < PIECES - 1:
                    acc[...] = d
                else:
                    put(d, 0)

        first = 1
    for n in range(first, end_tile):
        if load_p:
            arrive()

        @pl.when(place >= 0)
        def _(n=n):
            step(n)

    while ended[0] < len(units):
        arrive()


def partial_sums(solved, x, panel, span, orders, place, group, following, half, chips, within, extras):
    load_x, load_p = x is None, not isinstance(panel, list)
    panels = [in_hbm(panel)] if load_p else panel
    depth = solved.shape[1]
    block, low_row, width = span if load_p else (0, 0, sum(part.shape[0] for part in panel))
    count = len(group)
    rows = 2 * count * half
    tile = tile_of(width if load_p else panels[0].shape[0], 256)
    width = width // within[1]
    hbm, vmem = pl.BlockSpec(memory_space=pltpu.HBM), pl.BlockSpec(memory_space=pltpu.VMEM)
    operands = [place, in_hbm(solved)]
    in_specs = [pl.BlockSpec(memory_space=pltpu.SMEM), hbm]
    if not load_x:
        operands.append(x)
        in_specs.append(vmem)
    operands += panels
    in_specs += [hbm if load_p else vmem] * len(panels)
    operands += orders
    in_specs += [pl.BlockSpec(memory_space=pl.ANY)] * len(orders)
    operands += [in_hbm(array) for array, *_ in extras]
    in_specs += [hbm] * len(extras)
    shapes = [
        jax.ShapeDtypeStruct((count, half, width), BF16),
        jax.ShapeDtypeStruct((count, half, width), F32),
    ]
    if load_p:
        shapes.append(jax.ShapeDtypeStruct((span[2], depth), panel.dtype))
    if following:
        shapes.append(jax.ShapeDtypeStruct((2 * len(following) * half, depth), solved.dtype))
    shapes += [
        jax.ShapeDtypeStruct((size, array.shape[-1]), array.dtype) for array, _, _, size in extras
    ]
    scratch = [pltpu.VMEM((rows, depth), solved.dtype)] if load_x else []
    scratch.append(pltpu.VMEM((rows, tile), F32))
    copies = PIECES * (2 * count + 1) + panels[0].shape[-2] // tile + 2 * len(following) + PIECES * len(extras)
    scratch.append(pltpu.SemaphoreType.DMA((copies,)))
    cfg = (
        block, low_row, half, tile, load_p, load_x, tuple(group), tuple(following), len(orders),
        len(panels), within, tuple((layer, low) for _, layer, low, _ in extras), chips,
    )
    out = pl.pallas_call(
        functools.partial(partial_kernel, cfg),
        in_specs=in_specs,
        out_specs=[vmem] * len(shapes),
        out_shape=shapes,
        scratch_shapes=scratch,
        compiler_params=pltpu.CompilerParams(vmem_limit_bytes=LIMIT),
        cost_estimate=pl.CostEstimate(
            flops=2 * rows * width * depth,
            bytes_accessed=2 * depth * (rows + width),
            transcendentals=0,
        ),
    )(*operands)
    out = list(out)
    send, keep = out.pop(0), out.pop(0)
    held = [out.pop(0)] if load_p else []
    return send, keep, held, out.pop(0) if following else x, out


def residual(b, rhs_ref, parts, counts):
    total, parts = rhs_ref[:, b, :].astype(F32), list(parts)
    for count in counts:
        pieces = [parts.pop(0)[...].astype(F32) for _ in range(count)]
        total -= pieces[0] if count == 1 else jnp.concatenate(pieces, axis=1)
    return total


def blocks_of(mine, members, width):
    return [
        pl.ds(pl.multiple_of((mine ^ offset) * width, width), width)
        for offset in range(members)
    ]


def solve_first_kernel(counts, cols, place, rhs, *refs):
    count = sum(counts)
    parts, inverse, outs = refs[:count], refs[count], refs[count + 1 :]
    members, width = len(outs), rhs.shape[2]
    at = blocks_of(place[0] // cols, members, width)
    res = residual(0, rhs, parts, counts).astype(BF16)
    for offset in range(members - 1, -1, -1):
        d = jnp.dot(res, inverse[:, at[offset]], preferred_element_type=F32)
        outs[offset][...] = d.astype(outs[offset].dtype)


def carry(firsts, link, at, offsets):
    total = None
    for first, offset in zip(firsts, offsets):
        d = contract_last(first[...], link[:, at[offset]])
        total = d if total is None else total + d
    return total


def carry_kernel(members, offsets, cols, place, *refs):
    firsts, link, out = refs[:-3], refs[-3], refs[-1]
    at = blocks_of(place[0] // cols, members, out.shape[1])
    out[...] = carry(firsts, link, at, offsets)


def solve_second_kernel(counts, members, offsets, cols, place, rhs, *refs):
    count = sum(counts)
    parts, refs = refs[:count], refs[count:]
    early, refs = refs[0], refs[1:]
    firsts, refs = refs[: len(offsets)], refs[len(offsets) :]
    link, inverse, outs = refs[0], refs[1], refs[2:]
    at = blocks_of(place[0] // cols, members, rhs.shape[2])
    carried = early[...]
    if offsets:
        carried += carry(firsts, link, at, offsets)
    value = (residual(1, rhs, parts, counts) - carried).astype(BF16)
    for offset in range(members - 1, -1, -1):
        d = jnp.dot(value, inverse[:, at[offset]], preferred_element_type=F32)
        outs[offset][...] = d.astype(outs[offset].dtype)


def solve(kernel, flops, place, operands, shape, types):
    vmem = pl.BlockSpec(memory_space=pltpu.VMEM)
    return pl.pallas_call(
        kernel,
        in_specs=[pl.BlockSpec(memory_space=pltpu.SMEM)] + [vmem] * len(operands),
        out_specs=[vmem] * len(types),
        out_shape=[jax.ShapeDtypeStruct(shape, kind) for kind in types],
        compiler_params=pltpu.CompilerParams(vmem_limit_bytes=LIMIT),
        cost_estimate=pl.CostEstimate(
            flops=flops, bytes_accessed=flops // shape[0], transcendentals=0
        ),
    )(place, *operands)


def result_kernel(first, *refs):
    parts, out = refs[:-1], refs[-1]
    total = parts[0][...].astype(F32)
    for part in parts[1:]:
        total += part[...].astype(F32)
    out[:, 0, :] = first[...]
    out[:, 1, :] = total.astype(BF16)


def plan_of(chips):
    plan = [(0, [o], (0, 1)) for o in range(chips - 1, -1, -1)]
    plan += [(1, [o + 1, o], (0, 1)) for o in range(chips - 2, 0, -2)]
    return plan + [(1, [o], (0, 1)) for o in ([1, 0] if chips > 1 else [0])]


def deadline(plan, n, offset):
    odd, last = offset % 2, len(plan) - 1
    return min(last, n + (1 if plan[n][0] else 2 if odd else 3))


def local(members, chips, rhs, solved, panel, inverse, link):
    half, _, width = rhs.shape
    cols = 2 * chips
    place = lax.axis_index(("row", "col")).astype(jnp.int32)[None]

    def across_row(value, offset):
        return lax.ppermute(value, "row", [(i, i ^ offset) for i in range(members)])

    def across_col(value, offset):
        return lax.ppermute(value, "col", [(i, i ^ offset) for i in range(cols)])

    plan = plan_of(chips)
    last = len(plan) - 1

    extras = [[] for _ in plan]
    ahead = [n for n, (b, _, _) in enumerate(plan) if b == 0]
    extras[len(ahead) if last > len(ahead) + 1 else 0].append(("inverse", inverse, 0, 0, width))
    piece = width // 2
    extras[max(0, ahead[-1] - 2)].append(("low", panel, 1, 0, piece))
    extras[max(0, ahead[-1] - 1)].append(("high", panel, 1, piece, piece))
    extras[last - 1].append(("link", link, None, 0, width))
    extras[last].append(("second", inverse, 1, 0, width))

    flops = 2 * half * width * width * members
    kept, passing = {}, {}
    sums = [{}, {}]
    due = [[] for _ in plan]

    def term(b, key, value):
        sums[b].setdefault(key, []).append(value)

    def counts(b):
        return tuple(len(pieces) for pieces in sums[b].values())

    def flat(b):
        return [value for pieces in sums[b].values() for value in pieces]

    x, blocks = None, []
    for n, (b, group, part) in enumerate(plan):
        if n == len(ahead):
            blocks = [kept["low"], kept["high"]]
        follows = n < last and plan[n + 1][1] != group
        following = plan[n + 1][1] if follows else []
        orders = due[n]
        if n == last - 1:
            parts = solve(
                functools.partial(solve_first_kernel, counts(0), cols),
                flops, place, [rhs, *flat(0), kept["inverse"]],
                (half, width), [F32] + [BF16] * (members - 1),
            )
            orders = due[n] + [parts[members > 1]]
        if n == last:
            total = parts[0]
            for offset in range(1, members):
                total += across_row(parts[offset], offset).astype(F32)
            first = total.astype(BF16)
            orders = due[n] + [first]
        send, keep, held, x, got = partial_sums(
            solved, x, blocks if n else panel, (0, 0, width), orders, place,
            group, following, half, chips, part, [e[1:] for e in extras[n]],
        )
        blocks = blocks + held
        kept.update(zip([e[0] for e in extras[n]], got))
        other = across_col(send, 1)
        for at, offset in enumerate(group):
            if offset == 0:
                term(b, "own", keep[at])
                term(b, "swap", other[at])
                continue
            value = keep[at] + other[at].astype(F32)
            if offset % 2 == 0:
                value += passing.pop((b, offset)).astype(F32)
            value = value.astype(BF16)
            due[deadline(plan, n, offset)].append(value)
            arrived = across_col(value, 2 if offset % 2 else 2 * offset)
            if offset > 1 and offset % 2:
                passing[b, offset - 1] = arrived
            else:
                term(b, offset, arrived)

    firsts = [first] + [across_row(first, o) for o in range(1, members)]
    early = list(range(max(1, members - 1)))
    late = [o for o in range(members) if o not in early]
    vmem = pl.BlockSpec(memory_space=pltpu.VMEM)
    carried = pl.pallas_call(
        functools.partial(carry_kernel, members, early, cols),
        in_specs=[pl.BlockSpec(memory_space=pltpu.SMEM)] + [vmem] * (1 + len(early))
        + [pl.BlockSpec(memory_space=pl.ANY)],
        out_specs=vmem,
        out_shape=jax.ShapeDtypeStruct((half, width), F32),
        name="carry",
        compiler_params=pltpu.CompilerParams(vmem_limit_bytes=LIMIT),
        cost_estimate=pl.CostEstimate(
            flops=2 * half * width * width, bytes_accessed=width * width, transcendentals=0
        ),
    )(place, *[firsts[o] for o in early], kept["link"], keep)
    parts = solve(
        functools.partial(solve_second_kernel, counts(1), members, late, cols),
        2 * flops, place,
        [rhs, *flat(1), carried, *[firsts[o] for o in late], kept["link"], kept["second"]],
        (half, width), [F32] + [BF16] * (members - 1),
    )
    arrived = [across_row(parts[offset], offset) for offset in range(1, members)]
    return pl.pallas_call(
        result_kernel,
        out_shape=jax.ShapeDtypeStruct(rhs.shape, rhs.dtype),
        name="result",
        compiler_params=pltpu.CompilerParams(vmem_limit_bytes=LIMIT),
    )(first, parts[0], *arrived)


def solution(mesh):
    members, chips = mesh.shape["row"], mesh.shape["col"] // 2

    def body(*arrays):
        return local(members, chips, *arrays)

    return jax.shard_map(
        body,
        mesh=mesh,
        in_specs=(
            P("col", None, "row"),
            P(None, "col"),
            P(None, "row", "col"),
            P(None, "row", None),
            P("row", None),
        ),
        out_specs=P("col", None, "row"),
        check_vma=False,
    )
```

```python
import functools

import jax
import jax.numpy as jnp
from jax import lax
from jax.experimental import pallas as pl
from jax.experimental.pallas import tpu as pltpu
from jax.sharding import PartitionSpec as P


F32, BF16 = jnp.float32, jnp.bfloat16
AHEAD = 8
PIECES = 4
LIMIT = 6 << 20


def contract_last(a, b):
    return lax.dot_general(a, b, (((1,), (1,)), ((), ())), preferred_element_type=F32)


def tile_of(size, most):
    while size % most:
        most //= 2
    return most


def in_hbm(array):
    return pltpu.with_memory_space_constraint(array, pltpu.HBM)


def partial_kernel(cfg, *refs):
    block, low_row, half, tile, load_p, load_x, group, following, ordered, blocks, within, extras, chips = cfg
    refs = list(refs)
    place, solved = refs.pop(0)[0], refs.pop(0)
    x = None if load_x else refs.pop(0)
    held = [refs.pop(0) for _ in range(blocks)]
    panel = held[0]
    for _ in range(ordered):
        refs.pop(0)
    wanted = [refs.pop(0) for _ in extras]
    send, keep = refs.pop(0), refs.pop(0)
    if load_p:
        held = [refs.pop(0)]
    upcoming = refs.pop(0) if following else None
    fetched = [refs.pop(0) for _ in extras]
    if load_x:
        x = refs.pop(0)
    acc, sems = refs
    depth = solved.shape[1]
    piece = depth // PIECES
    per = held[0].shape[0] // tile
    tiles = per * len(held)
    begin_tile, end_tile = [tiles * edge // within[1] for edge in (within[0], within[0] + 1)]
    count = len(group)
    chip, core = lax.rem(place, 2 * chips) // 2, lax.rem(place, 2)
    used = [0]

    def copy(source, target):
        used[0] += 1
        return pltpu.make_async_copy(source, target, sems.at[used[0] - 1])

    def rows_copy(offsets, target, at, columns):
        parity = 1 - core if at < len(offsets) else core
        start = ((chip ^ offsets[at % len(offsets)]) * 2 + parity) * half
        return copy(
            solved.at[pl.ds(pl.multiple_of(start, half), half), columns],
            target.at[pl.ds(at * half, half), columns],
        )

    def panel_copy(n, columns):
        rows = pl.ds(n * tile, tile)
        return copy(panel.at[block, pl.ds(low_row + n * tile, tile), columns], held[0].at[rows, columns])

    units = []
    if load_x or load_p:
        for j in range(PIECES):
            columns = pl.ds(j * piece, piece)
            unit = [rows_copy(group, x, s, columns) for s in range(2 * count)] if load_x else []
            units.append(unit + ([panel_copy(0, columns)] if load_p else []))
    if load_p:
        units += [[panel_copy(n, slice(None))] for n in range(1, tiles)]
    units += [[rows_copy(following, upcoming, s, slice(None))] for s in range(2 * len(following))]
    for (layer, low), source, target in zip(extras, wanted, fetched):
        step = target.shape[0] // PIECES
        for j in range(PIECES):
            rows = pl.ds(low + j * step, step)
            part = source.at[rows] if layer is None else source.at[layer, rows]
            units.append([copy(part, target.at[pl.ds(j * step, step)])])
    ahead = AHEAD if load_p else len(units)
    begun, ended = [0], [0]

    def begin():
        while begun[0] < min(ended[0] + ahead, len(units)):
            for c in units[begun[0]]:
                c.start()
            begun[0] += 1

    def arrive():
        begin()
        for c in units[ended[0]]:
            c.wait()
        ended[0] += 1
        begin()

    begin()

    def put(d, n):
        at = pl.ds((n - begin_tile) * tile, tile)
        for c in range(count):
            send[c, :, at] = d[c * half : (c + 1) * half].astype(send.dtype)
            keep[c, :, at] = d[(count + c) * half : (count + c + 1) * half]

    def step(n):
        put(contract_last(x[...], held[n // per][pl.ds(n % per * tile, tile), :]), n)

    first = begin_tile
    if load_x or load_p:
        for j in range(PIECES):
            arrive()

            @pl.when(place >= 0)
            def _(j=j):
                columns = pl.ds(j * piece, piece)
                d = contract_last(x[:, columns], held[0][pl.ds(0, tile), columns])
                if j > 0:
                    d = acc[...] + d
                if j < PIECES - 1:
                    acc[...] = d
                else:
                    put(d, 0)

        first = 1
    for n in range(first, end_tile):
        if load_p:
            arrive()

        @pl.when(place >= 0)
        def _(n=n):
            step(n)

    while ended[0] < len(units):
        arrive()


def partial_sums(solved, x, panel, span, orders, place, group, following, half, chips, within, extras):
    load_x, load_p = x is None, not isinstance(panel, list)
    panels = [in_hbm(panel)] if load_p else panel
    depth = solved.shape[1]
    block, low_row, width = span if load_p else (0, 0, sum(part.shape[0] for part in panel))
    count = len(group)
    rows = 2 * count * half
    tile = tile_of(width if load_p else panels[0].shape[0], 256)
    width = width // within[1]
    hbm, vmem = pl.BlockSpec(memory_space=pltpu.HBM), pl.BlockSpec(memory_space=pltpu.VMEM)
    operands = [place, in_hbm(solved)]
    in_specs = [pl.BlockSpec(memory_space=pltpu.SMEM), hbm]
    if not load_x:
        operands.append(x)
        in_specs.append(vmem)
    operands += panels
    in_specs += [hbm if load_p else vmem] * len(panels)
    operands += orders
    in_specs += [pl.BlockSpec(memory_space=pl.ANY)] * len(orders)
    operands += [in_hbm(array) for array, *_ in extras]
    in_specs += [hbm] * len(extras)
    shapes = [
        jax.ShapeDtypeStruct((count, half, width), BF16),
        jax.ShapeDtypeStruct((count, half, width), F32),
    ]
    if load_p:
        shapes.append(jax.ShapeDtypeStruct((span[2], depth), panel.dtype))
    if following:
        shapes.append(jax.ShapeDtypeStruct((2 * len(following) * half, depth), solved.dtype))
    shapes += [
        jax.ShapeDtypeStruct((size, array.shape[-1]), array.dtype) for array, _, _, size in extras
    ]
    scratch = [pltpu.VMEM((rows, depth), solved.dtype)] if load_x else []
    scratch.append(pltpu.VMEM((rows, tile), F32))
    copies = PIECES * (2 * count + 1) + panels[0].shape[-2] // tile + 2 * len(following) + PIECES * len(extras)
    scratch.append(pltpu.SemaphoreType.DMA((copies,)))
    cfg = (
        block, low_row, half, tile, load_p, load_x, tuple(group), tuple(following), len(orders),
        len(panels), within, tuple((layer, low) for _, layer, low, _ in extras), chips,
    )
    out = pl.pallas_call(
        functools.partial(partial_kernel, cfg),
        in_specs=in_specs,
        out_specs=[vmem] * len(shapes),
        out_shape=shapes,
        scratch_shapes=scratch,
        compiler_params=pltpu.CompilerParams(vmem_limit_bytes=LIMIT),
        cost_estimate=pl.CostEstimate(
            flops=2 * rows * width * depth,
            bytes_accessed=2 * depth * (rows + width),
            transcendentals=0,
        ),
    )(*operands)
    out = list(out)
    send, keep = out.pop(0), out.pop(0)
    held = [out.pop(0)] if load_p else []
    return send, keep, held, out.pop(0) if following else x, out


def residual(b, rhs_ref, parts, counts):
    total, parts = rhs_ref[:, b, :].astype(F32), list(parts)
    for count in counts:
        pieces = [parts.pop(0)[...].astype(F32) for _ in range(count)]
        total -= pieces[0] if count == 1 else jnp.concatenate(pieces, axis=1)
    return total


def blocks_of(mine, members, width):
    return [
        pl.ds(pl.multiple_of((mine ^ offset) * width, width), width)
        for offset in range(members)
    ]


def solve_first_kernel(counts, cols, place, rhs, *refs):
    count = sum(counts)
    parts, inverse, outs = refs[:count], refs[count], refs[count + 1 :]
    members, width = len(outs), rhs.shape[2]
    at = blocks_of(place[0] // cols, members, width)
    res = residual(0, rhs, parts, counts).astype(BF16)
    for offset in range(members - 1, -1, -1):
        d = jnp.dot(res, inverse[:, at[offset]], preferred_element_type=F32)
        outs[offset][...] = d.astype(outs[offset].dtype)


def carry(firsts, link, at, offsets):
    total = None
    for first, offset in zip(firsts, offsets):
        d = contract_last(first[...], link[:, at[offset]])
        total = d if total is None else total + d
    return total


def carry_kernel(members, offsets, cols, place, *refs):
    firsts, link, out = refs[:-3], refs[-3], refs[-1]
    at = blocks_of(place[0] // cols, members, out.shape[1])
    out[...] = carry(firsts, link, at, offsets)


def solve_second_kernel(counts, members, offsets, cols, place, rhs, *refs):
    count = sum(counts)
    parts, refs = refs[:count], refs[count:]
    early, refs = refs[0], refs[1:]
    firsts, refs = refs[: len(offsets)], refs[len(offsets) :]
    link, inverse, outs = refs[0], refs[1], refs[2:]
    at = blocks_of(place[0] // cols, members, rhs.shape[2])
    carried = early[...]
    if offsets:
        carried += carry(firsts, link, at, offsets)
    value = (residual(1, rhs, parts, counts) - carried).astype(BF16)
    for offset in range(members - 1, -1, -1):
        d = jnp.dot(value, inverse[:, at[offset]], preferred_element_type=F32)
        outs[offset][...] = d.astype(outs[offset].dtype)


def solve(kernel, flops, place, operands, shape, types):
    vmem = pl.BlockSpec(memory_space=pltpu.VMEM)
    return pl.pallas_call(
        kernel,
        in_specs=[pl.BlockSpec(memory_space=pltpu.SMEM)] + [vmem] * len(operands),
        out_specs=[vmem] * len(types),
        out_shape=[jax.ShapeDtypeStruct(shape, kind) for kind in types],
        compiler_params=pltpu.CompilerParams(vmem_limit_bytes=LIMIT),
        cost_estimate=pl.CostEstimate(
            flops=flops, bytes_accessed=flops // shape[0], transcendentals=0
        ),
    )(place, *operands)


def result_kernel(first, *refs):
    parts, out = refs[:-1], refs[-1]
    total = parts[0][...].astype(F32)
    for part in parts[1:]:
        total += part[...].astype(F32)
    out[:, 0, :] = first[...]
    out[:, 1, :] = total.astype(BF16)


def plan_of(chips):
    order = [chips - 1] + [o + step for o in range(chips - 3, 0, -2) for step in (0, 1)]
    plan = [(0, [o], (0, 1)) for o in order + ([0] if chips > 1 else [])]
    plan += [(1, [o + 1, o], (0, 1)) for o in range(chips - 2, 0, -2)]
    return plan + [(1, [o], (0, 1)) for o in ([1, 0] if chips > 1 else [0])]


def deadline(plan, n):
    return min(len(plan) - 1, n + (1 if plan[n][0] else 2))


def local(members, chips, rhs, solved, panel, inverse, link):
    half, _, width = rhs.shape
    cols = 2 * chips
    place = lax.axis_index(("row", "col")).astype(jnp.int32)[None]

    def across_row(value, offset):
        return lax.ppermute(value, "row", [(i, i ^ offset) for i in range(members)])

    def across_col(value, offset):
        return lax.ppermute(value, "col", [(i, i ^ offset) for i in range(cols)])

    plan = plan_of(chips)
    last = len(plan) - 1

    extras = [[] for _ in plan]
    ahead = [n for n, (b, _, _) in enumerate(plan) if b == 0]
    extras[len(ahead) if last > len(ahead) + 1 else 0].append(("inverse", inverse, 0, 0, width))
    piece = width // 2
    extras[max(0, ahead[-1] - 2)].append(("low", panel, 1, 0, piece))
    extras[max(0, ahead[-1] - 1)].append(("high", panel, 1, piece, piece))
    extras[last - 1].append(("link", link, None, 0, width))
    extras[last].append(("second", inverse, 1, 0, width))

    flops = 2 * half * width * width * members
    kept, passing = {}, {}
    sums = [{}, {}]
    due = [[] for _ in plan]

    def term(b, key, value):
        sums[b].setdefault(key, []).append(value)

    def counts(b):
        return tuple(len(pieces) for pieces in sums[b].values())

    def flat(b):
        return [value for pieces in sums[b].values() for value in pieces]

    x, blocks = None, []
    for n, (b, group, part) in enumerate(plan):
        if n == len(ahead):
            blocks = [kept["low"], kept["high"]]
        follows = n < last and plan[n + 1][1] != group
        following = plan[n + 1][1] if follows else []
        orders = due[n]
        if n == last - 1:
            parts = solve(
                functools.partial(solve_first_kernel, counts(0), cols),
                flops, place, [rhs, *flat(0), kept["inverse"]],
                (half, width), [F32] + [BF16] * (members - 1),
            )
            orders = due[n] + [parts[members > 1]]
        if n == last:
            total = parts[0]
            for offset in range(1, members):
                total += across_row(parts[offset], offset).astype(F32)
            first = total.astype(BF16)
            orders = due[n] + [first]
        send, keep, held, x, got = partial_sums(
            solved, x, blocks if n else panel, (0, 0, width), orders, place,
            group, following, half, chips, part, [e[1:] for e in extras[n]],
        )
        blocks = blocks + held
        kept.update(zip([e[0] for e in extras[n]], got))
        other = across_col(send, 1)
        for at, offset in enumerate(group):
            if offset == 0:
                term(b, "own", keep[at])
                term(b, "swap", other[at])
                continue
            value = keep[at] + other[at].astype(F32)
            if offset % 2 == 0:
                value += passing.pop((b, offset)).astype(F32)
            value = value.astype(BF16)
            due[deadline(plan, n) if b == 0 or offset % 2 else last].append(value)
            arrived = across_col(value, 2 if offset % 2 else 2 * offset)
            if offset > 1 and offset % 2:
                passing[b, offset - 1] = arrived
            else:
                term(b, offset, arrived)

    firsts = [first] + [across_row(first, o) for o in range(1, members)]
    early = list(range(max(1, members - 1)))
    late = [o for o in range(members) if o not in early]
    vmem = pl.BlockSpec(memory_space=pltpu.VMEM)
    carried = pl.pallas_call(
        functools.partial(carry_kernel, members, early, cols),
        in_specs=[pl.BlockSpec(memory_space=pltpu.SMEM)] + [vmem] * (1 + len(early))
        + [pl.BlockSpec(memory_space=pl.ANY)],
        out_specs=vmem,
        out_shape=jax.ShapeDtypeStruct((half, width), F32),
        name="carry",
        compiler_params=pltpu.CompilerParams(vmem_limit_bytes=LIMIT),
        cost_estimate=pl.CostEstimate(
            flops=2 * half * width * width, bytes_accessed=width * width, transcendentals=0
        ),
    )(place, *[firsts[o] for o in early], kept["link"], keep)
    parts = solve(
        functools.partial(solve_second_kernel, counts(1), members, late, cols),
        2 * flops, place,
        [rhs, *flat(1), carried, *[firsts[o] for o in late], kept["link"], kept["second"]],
        (half, width), [F32] + [BF16] * (members - 1),
    )
    arrived = [across_row(parts[offset], offset) for offset in range(1, members)]
    return pl.pallas_call(
        result_kernel,
        out_shape=jax.ShapeDtypeStruct(rhs.shape, rhs.dtype),
        name="result",
        compiler_params=pltpu.CompilerParams(vmem_limit_bytes=LIMIT),
    )(first, parts[0], *arrived)


def solution(mesh):
    members, chips = mesh.shape["row"], mesh.shape["col"] // 2

    def body(*arrays):
        return local(members, chips, *arrays)

    return jax.shard_map(
        body,
        mesh=mesh,
        in_specs=(
            P("col", None, "row"),
            P(None, "col"),
            P(None, "row", "col"),
            P(None, "row", None),
            P("row", None),
        ),
        out_specs=P("col", None, "row"),
        check_vma=False,
    )
```
